256 devices in a mesh: dom: 16 (over y, z_lo, core), dir: 16 (over x, z_hi).
Axes of the slice: x: 4, y: 4, z: 8 (z_hi: 4, z_lo: 2; z = z_hi * 2 + z_lo), core: 2. Of those that a mesh axis runs over, the one named last changes fastest.
Arguments:
- coefficients: bfloat16 [2, 70, 32768], P(None, None, ('dom', 'dir')), may hold values from -6 to 6
- positions: float32 [3, 32768], P(None, ('dom', 'dir')), may hold values from -50 to 50
- polar: float32 [10240], P('dir'), may hold values from 0 to 1.4
- azimuth: float32 [10240], P('dir'), may hold values from -3.140625 to 3.140625
- weights: float32 [10240], P('dir'), may hold values from -4 to 4
- farmap: float32 [2, 2, 70, 10240], P(None, None, None, 'dir'), may hold values from -0.00390625 to 0.00390625
Outputs:
- coef_grad: float32 [2, 70, 32768], P(None, None, ('dom', 'dir'))
- place_grad: float32 [3, 32768], P(None, ('dom', 'dir'))
The draws below stay inside these ranges and needn't reach their ends.
All inputs are finite; a program needn't handle non-finite values.
Results may differ from the reference program's by a relative error of at most 0.0052.
Values may be sent and summed in bfloat16 or wider, within the bound.
A program may use at most 64 MiB of HBM per device.

```python
import jax
import jax.numpy as jnp
from jax import lax

C = 70
P_SIZE = 32768
K = 10240


def steps_of(rng, extent, cuts, smallest, top_value):
    factor_of = 1.0
    for position, blocks in cuts:
        draws = jax.random.uniform(jax.random.fold_in(jax.random.fold_in(rng, 6), position), (blocks,), jnp.float32, smallest / len(cuts), top_value / len(cuts))
        factor_of = factor_of * jnp.repeat(jnp.exp(draws), extent[position] // blocks).reshape((-1,) + (1,) * (len(extent) - 1 - position))
    return factor_of


def centred(own_key, dims, scale, reach, split=(), kind=jnp.bfloat16):
    drawn = jax.random.normal(own_key, dims, jnp.float32) * scale
    if len(split) > 0:
        drawn = steps_of(own_key, dims, split, -0.22, 0.18) * drawn
    return jnp.clip(drawn, min=-reach, max=reach).astype(kind)


def setup_inputs(seed: int = 0) -> dict:
    keys = jax.random.split(jax.random.key(seed), 7)
    return {
        "coefficients": centred(keys[0], (2, C, P_SIZE), 1.0, 6.0, ((2, 256),)),
        "positions": jnp.clip(jax.random.uniform(keys[1], (3, P_SIZE), jnp.float32, -50.0, 50.0) * steps_of(keys[1], (3, P_SIZE), ((1, 256),), -0.4, 0.0), -50.0, 50.0),
        "polar": jnp.clip(1.4 * jax.random.uniform(keys[2], (K,), jnp.float32) ** steps_of(keys[2], (K,), ((0, 16),), -0.2, 0.2), 0.0, 1.4),
        "azimuth": jnp.clip(jax.random.uniform(keys[3], (K,), jnp.float32, -3.140625, 3.140625), -3.140625, 3.140625),
        "weights": jnp.clip(jax.random.uniform(keys[4], (K,), jnp.float32, -4.0, 4.0) * steps_of(keys[4], (K,), ((0, 16),), -0.4, 0.0), -4.0, 4.0),
        "farmap": centred(keys[5], (2, 2, C, K), (C * P_SIZE) ** -0.5, 0.00390625, ((3, 16),), jnp.float32),
    }


def unit_vectors(polar, azimuth):
    sine_polar = jnp.sin(polar)
    return jnp.stack([sine_polar * jnp.cos(azimuth), sine_polar * jnp.sin(azimuth), jnp.cos(polar)])


def phase_tile(places, vectors):
    angles = places[0][:, None] * vectors[0][None, :] + places[1][:, None] * vectors[1][None, :] + places[2][:, None] * vectors[2][None, :]
    return jnp.cos(angles).astype(jnp.bfloat16), jnp.sin(angles).astype(jnp.bfloat16)


def field_terms(coef_block, cos_tile, sin_tile):
    order_count = coef_block.shape[0] // 2
    real_rows = coef_block[:order_count]
    imag_rows = coef_block[order_count:]
    top_rows = jnp.concatenate([real_rows, imag_rows], axis=1)
    low_rows = jnp.concatenate([imag_rows, -real_rows], axis=1)
    left_side = jnp.concatenate([top_rows, low_rows], axis=0).astype(jnp.float32)
    right_side = jnp.concatenate([cos_tile, sin_tile], axis=0).astype(jnp.float32)
    return jnp.dot(left_side, right_side, preferred_element_type=jnp.float32)


def adjoint_terms(stacked, cos_tile, sin_tile):
    order_count = stacked.shape[0] // 2
    real_rows = stacked[:order_count]
    imag_rows = stacked[order_count:]
    top_rows = jnp.concatenate([real_rows, imag_rows], axis=1)
    low_rows = jnp.concatenate([imag_rows, -real_rows], axis=1)
    left_side = jnp.concatenate([top_rows, low_rows], axis=0).astype(jnp.float32)
    right_side = jnp.concatenate([cos_tile, sin_tile], axis=1).astype(jnp.float32)
    return lax.dot_general(left_side, right_side, (((1,), (1,)), ((), ())), preferred_element_type=jnp.float32)


def cotangent_rows(fields, farmap, weights):
    order_count = fields.shape[0] // 2
    field_real = fields[:order_count][None]
    field_imag = fields[order_count:][None]
    map_real = farmap[:, 0]
    map_imag = farmap[:, 1]
    amp_real = jnp.sum(map_real * field_real - map_imag * field_imag, axis=1)
    amp_imag = jnp.sum(map_real * field_imag + map_imag * field_real, axis=1)
    cot_real = weights * jnp.sum(amp_real[:, None] * map_real + amp_imag[:, None] * map_imag, axis=0)
    cot_imag = weights * jnp.sum(amp_real[:, None] * map_imag - amp_imag[:, None] * map_real, axis=0)
    return jnp.concatenate([cot_real, cot_imag], axis=0).astype(jnp.bfloat16)


def stacked_rows(adjoint, vectors):
    order_count = adjoint.shape[0] // 2
    widened = adjoint.astype(jnp.float32)
    scaled = [(vectors[axis_id][None, :] * widened).astype(jnp.bfloat16) for axis_id in range(3)]
    real_parts = [adjoint[:order_count]] + [item[:order_count] for item in scaled]
    imag_parts = [adjoint[order_count:]] + [item[order_count:] for item in scaled]
    return jnp.concatenate(real_parts + imag_parts, axis=0)


def gradients(output, coef_block):
    order_count = coef_block.shape[0] // 2
    real_out = output[:4 * order_count]
    imag_out = output[4 * order_count:]
    coef_term = jnp.concatenate([2.0 * real_out[:order_count], -2.0 * imag_out[:order_count]], axis=0)
    coef_real = coef_block[:order_count].astype(jnp.float32)
    coef_imag = coef_block[order_count:].astype(jnp.float32)
    place_terms = []
    for axis_id in range(3):
        lower_row = (axis_id + 1) * order_count
        upper_row = (axis_id + 2) * order_count
        place_terms.append(2.0 * jnp.sum(coef_real * imag_out[lower_row:upper_row] + coef_imag * real_out[lower_row:upper_row], axis=0))
    return coef_term, jnp.stack(place_terms)


def reference(coefficients, positions, polar, azimuth, weights, farmap):
    vectors = unit_vectors(polar, azimuth)
    coef_rows = coefficients.reshape(2 * C, P_SIZE)
    width_block = 512 if P_SIZE % 512 == 0 else P_SIZE
    blocks = P_SIZE // width_block

    def forward_block(totals, block_id):
        offset = (block_id * width_block).astype(jnp.int32)
        coef_block = lax.dynamic_slice_in_dim(coef_rows, offset, width_block, 1)
        place_block = lax.dynamic_slice_in_dim(positions, offset, width_block, 1)
        cos_tile, sin_tile = phase_tile(place_block, vectors)
        return totals + field_terms(coef_block, cos_tile, sin_tile), None

    fields, _ = lax.scan(forward_block, jnp.zeros((2 * C, K), jnp.float32), jnp.arange(blocks, dtype=jnp.int32))
    adjoint = cotangent_rows(fields, farmap, weights)
    stacked = stacked_rows(adjoint, vectors)

    def backward_block(block_id):
        offset = (block_id * width_block).astype(jnp.int32)
        coef_block = lax.dynamic_slice_in_dim(coef_rows, offset, width_block, 1)
        place_block = lax.dynamic_slice_in_dim(positions, offset, width_block, 1)
        cos_tile, sin_tile = phase_tile(place_block, vectors)
        return gradients(adjoint_terms(stacked, cos_tile, sin_tile), coef_block)

    coef_parts, place_parts = lax.map(backward_block, jnp.arange(blocks, dtype=jnp.int32))
    coef_grad = jnp.moveaxis(coef_parts, 0, 1).reshape(2, C, P_SIZE)
    place_grad = jnp.moveaxis(place_parts, 0, 1).reshape(3, P_SIZE)
    return coef_grad, place_grad
```

```python
import functools

import jax
import jax.numpy as jnp
from jax import lax
from jax.sharding import PartitionSpec as P

C = 70


def unit_vectors(polar, azimuth):
    sine_polar = jnp.sin(polar)
    return jnp.stack([sine_polar * jnp.cos(azimuth), sine_polar * jnp.sin(azimuth), jnp.cos(polar)])


def phase_tile(places, vectors):
    angles = (
        places[0][:, None] * vectors[0][None, :]
        + places[1][:, None] * vectors[1][None, :]
        + places[2][:, None] * vectors[2][None, :]
    )
    return (jnp.cos(angles).astype(jnp.bfloat16), jnp.sin(angles).astype(jnp.bfloat16))


def field_terms(coef_block, cos_tile, sin_tile):
    order_count = coef_block.shape[0] // 2
    real_rows = coef_block[:order_count]
    imag_rows = coef_block[order_count:]
    top_rows = jnp.concatenate([real_rows, imag_rows], axis=1)
    low_rows = jnp.concatenate([imag_rows, -real_rows], axis=1)
    left_side = jnp.concatenate([top_rows, low_rows], axis=0)
    right_side = jnp.concatenate([cos_tile, sin_tile], axis=0)
    return jnp.dot(left_side, right_side, preferred_element_type=jnp.float32)


def adjoint_terms(stacked, cos_tile, sin_tile):
    order_count = stacked.shape[0] // 2
    real_rows = stacked[:order_count]
    imag_rows = stacked[order_count:]
    top_rows = jnp.concatenate([real_rows, imag_rows], axis=1)
    low_rows = jnp.concatenate([imag_rows, -real_rows], axis=1)
    left_side = jnp.concatenate([top_rows, low_rows], axis=0)
    right_side = jnp.concatenate([cos_tile, sin_tile], axis=1)
    return lax.dot_general(
        left_side, right_side, (((1,), (1,)), ((), ())), preferred_element_type=jnp.float32
    )


def amplitude_parts(fields, farmap):
    order_count = fields.shape[0] // 2
    field_real = fields[:order_count][None]
    field_imag = fields[order_count:][None]
    map_real = farmap[:, 0]
    map_imag = farmap[:, 1]
    amp_real = jnp.sum(map_real * field_real - map_imag * field_imag, axis=1)
    amp_imag = jnp.sum(map_real * field_imag + map_imag * field_real, axis=1)
    return (amp_real, amp_imag)


def cotangent_from(amp_real, amp_imag, farmap, weights):
    map_real = farmap[:, 0]
    map_imag = farmap[:, 1]
    cot_real = weights * jnp.sum(
        amp_real[:, None] * map_real + amp_imag[:, None] * map_imag, axis=0
    )
    cot_imag = weights * jnp.sum(
        amp_real[:, None] * map_imag - amp_imag[:, None] * map_real, axis=0
    )
    return jnp.concatenate([cot_real, cot_imag], axis=0).astype(jnp.bfloat16)


def cotangent_rows(fields, farmap, weights):
    amp_real, amp_imag = amplitude_parts(fields, farmap)
    return cotangent_from(amp_real, amp_imag, farmap, weights)


def stacked_rows(adjoint, vectors):
    order_count = adjoint.shape[0] // 2
    widened = adjoint.astype(jnp.float32)
    scaled = [(vectors[axis_id][None, :] * widened).astype(jnp.bfloat16) for axis_id in range(3)]
    real_parts = [adjoint[:order_count]] + [item[:order_count] for item in scaled]
    imag_parts = [adjoint[order_count:]] + [item[order_count:] for item in scaled]
    return jnp.concatenate(real_parts + imag_parts, axis=0)


def gradients(output, coef_block):
    order_count = coef_block.shape[0] // 2
    real_out = output[: 4 * order_count]
    imag_out = output[4 * order_count :]
    coef_term = jnp.concatenate(
        [2.0 * real_out[:order_count], -2.0 * imag_out[:order_count]], axis=0
    )
    coef_real = coef_block[:order_count].astype(jnp.float32)
    coef_imag = coef_block[order_count:].astype(jnp.float32)
    place_terms = []
    for axis_id in range(3):
        lower_row = (axis_id + 1) * order_count
        upper_row = (axis_id + 2) * order_count
        place_terms.append(
            2.0
            * jnp.sum(
                coef_real * imag_out[lower_row:upper_row]
                + coef_imag * real_out[lower_row:upper_row],
                axis=0,
            )
        )
    return (coef_term, jnp.stack(place_terms))


def xor_pairs(size, mask):
    return [(index, index ^ mask) for index in range(size)]


def step_masks(size, nearest_last):
    masks = [1 << bit for bit in range(size.bit_length() - 1)]
    assert 1 << len(masks) == size
    if nearest_last and size == 16:
        masks = [2, 8, 1, 4]
    return masks


def body(coefficients, positions, polar, azimuth, weights, farmap, dir_size, dom_size):
    own_count = coefficients.shape[2]
    dir_masks = step_masks(dir_size, True)
    dom_masks = step_masks(dom_size, False)
    own_rows = jnp.concatenate(
        [coefficients.reshape(2 * C, own_count).astype(jnp.float32), positions], axis=0
    )
    gathered = own_rows
    for mask in dir_masks:
        gathered = jnp.concatenate(
            [gathered, lax.ppermute(gathered, "dir", xor_pairs(dir_size, mask))], axis=1
        )
    domain_rows = gathered[: 2 * C].astype(jnp.bfloat16)
    domain_places = gathered[2 * C :]
    vectors = unit_vectors(polar, azimuth)
    cos_tile, sin_tile = phase_tile(domain_places, vectors)
    fields = field_terms(domain_rows, cos_tile, sin_tile)
    for mask in dom_masks:
        fields = fields + lax.ppermute(fields, "dom", xor_pairs(dom_size, mask))
    adjoint = cotangent_rows(fields, farmap, weights)
    stacked = stacked_rows(adjoint, vectors)
    coef_part, place_part = gradients(adjoint_terms(stacked, cos_tile, sin_tile), domain_rows)
    part = jnp.concatenate([coef_part, place_part], axis=0)
    for step in reversed(range(len(dir_masks))):
        half = own_count << step
        received = lax.ppermute(
            part[:, half : 2 * half], "dir", xor_pairs(dir_size, dir_masks[step])
        )
        part = part[:, :half] + received
    return (part[: 2 * C].reshape(2, C, own_count), part[2 * C :])


def solution(mesh):
    placed = (
        P(None, None, ("dom", "dir")),
        P(None, ("dom", "dir")),
        P("dir"),
        P("dir"),
        P("dir"),
        P(None, None, None, "dir"),
    )
    return jax.shard_map(
        functools.partial(body, dir_size=mesh.shape["dir"], dom_size=mesh.shape["dom"]),
        mesh=mesh,
        in_specs=placed,
        out_specs=(P(None, None, ("dom", "dir")), P(None, ("dom", "dir"))),
        check_vma=False,
    )
```

```python
import functools

import jax
import jax.numpy as jnp
from jax import lax
from jax.sharding import PartitionSpec as P

C = 70


def unit_vectors(polar, azimuth):
    sine_polar = jnp.sin(polar)
    return jnp.stack([sine_polar * jnp.cos(azimuth), sine_polar * jnp.sin(azimuth), jnp.cos(polar)])


def phase_tile(places, vectors):
    angles = (
        places[0][:, None] * vectors[0][None, :]
        + places[1][:, None] * vectors[1][None, :]
        + places[2][:, None] * vectors[2][None, :]
    )
    return (jnp.cos(angles).astype(jnp.bfloat16), jnp.sin(angles).astype(jnp.bfloat16))


def field_terms(coef_block, cos_tile, sin_tile):
    order_count = coef_block.shape[0] // 2
    real_rows = coef_block[:order_count]
    imag_rows = coef_block[order_count:]
    top_rows = jnp.concatenate([real_rows, imag_rows], axis=1)
    low_rows = jnp.concatenate([imag_rows, -real_rows], axis=1)
    left_side = jnp.concatenate([top_rows, low_rows], axis=0)
    right_side = jnp.concatenate([cos_tile, sin_tile], axis=0)
    return jnp.dot(left_side, right_side, preferred_element_type=jnp.float32)


def adjoint_terms(stacked, cos_tile, sin_tile):
    order_count = stacked.shape[0] // 2
    real_rows = stacked[:order_count]
    imag_rows = stacked[order_count:]
    top_rows = jnp.concatenate([real_rows, imag_rows], axis=1)
    low_rows = jnp.concatenate([imag_rows, -real_rows], axis=1)
    left_side = jnp.concatenate([top_rows, low_rows], axis=0)
    right_side = jnp.concatenate([cos_tile, sin_tile], axis=1)
    return lax.dot_general(
        left_side, right_side, (((1,), (1,)), ((), ())), preferred_element_type=jnp.float32
    )


def amplitude_parts(fields, farmap):
    order_count = fields.shape[0] // 2
    field_real = fields[:order_count][None]
    field_imag = fields[order_count:][None]
    map_real = farmap[:, 0]
    map_imag = farmap[:, 1]
    amp_real = jnp.sum(map_real * field_real - map_imag * field_imag, axis=1)
    amp_imag = jnp.sum(map_real * field_imag + map_imag * field_real, axis=1)
    return (amp_real, amp_imag)


def cotangent_from(amp_real, amp_imag, farmap, weights):
    map_real = farmap[:, 0]
    map_imag = farmap[:, 1]
    cot_real = weights * jnp.sum(
        amp_real[:, None] * map_real + amp_imag[:, None] * map_imag, axis=0
    )
    cot_imag = weights * jnp.sum(
        amp_real[:, None] * map_imag - amp_imag[:, None] * map_real, axis=0
    )
    return jnp.concatenate([cot_real, cot_imag], axis=0).astype(jnp.bfloat16)


def cotangent_rows(fields, farmap, weights):
    amp_real, amp_imag = amplitude_parts(fields, farmap)
    return cotangent_from(amp_real, amp_imag, farmap, weights)


def stacked_rows(adjoint, vectors):
    order_count = adjoint.shape[0] // 2
    widened = adjoint.astype(jnp.float32)
    scaled = [(vectors[axis_id][None, :] * widened).astype(jnp.bfloat16) for axis_id in range(3)]
    real_parts = [adjoint[:order_count]] + [item[:order_count] for item in scaled]
    imag_parts = [adjoint[order_count:]] + [item[order_count:] for item in scaled]
    return jnp.concatenate(real_parts + imag_parts, axis=0)


def gradients(output, coef_block):
    order_count = coef_block.shape[0] // 2
    real_out = output[: 4 * order_count]
    imag_out = output[4 * order_count :]
    coef_term = jnp.concatenate(
        [2.0 * real_out[:order_count], -2.0 * imag_out[:order_count]], axis=0
    )
    coef_real = coef_block[:order_count].astype(jnp.float32)
    coef_imag = coef_block[order_count:].astype(jnp.float32)
    place_terms = []
    for axis_id in range(3):
        lower_row = (axis_id + 1) * order_count
        upper_row = (axis_id + 2) * order_count
        place_terms.append(
            2.0
            * jnp.sum(
                coef_real * imag_out[lower_row:upper_row]
                + coef_imag * real_out[lower_row:upper_row],
                axis=0,
            )
        )
    return (coef_term, jnp.stack(place_terms))


def gather_blocks(block, axis_name, size):
    spread = jnp.broadcast_to(block[None], (size,) + block.shape)
    return lax.all_to_all(spread, axis_name, 0, 0, tiled=True)


def scatter_sum(part, axis_name, size):
    rows, width = part.shape
    split = part.reshape(rows, size, width // size)
    received = lax.all_to_all(split, axis_name, 1, 1, tiled=True)
    return jnp.sum(received, axis=1)


def body(coefficients, positions, polar, azimuth, weights, farmap, dir_size, dom_size):
    own_count = coefficients.shape[2]
    own_rows = coefficients.reshape(2 * C, own_count)
    coef_blocks = gather_blocks(own_rows, "dir", dir_size)
    place_blocks = gather_blocks(positions, "dir", dir_size)
    domain_rows = jnp.moveaxis(coef_blocks, 0, 1).reshape(2 * C, dir_size * own_count)
    domain_places = jnp.moveaxis(place_blocks, 0, 1).reshape(3, dir_size * own_count)
    vectors = unit_vectors(polar, azimuth)
    cos_tile, sin_tile = phase_tile(domain_places, vectors)
    partial_fields = field_terms(domain_rows, cos_tile, sin_tile)
    dir_count = polar.shape[0]
    slice_width = dir_count // dom_size
    fields_slice = scatter_sum(partial_fields, "dom", dom_size)
    offset = lax.axis_index("dom") * slice_width
    farmap_slice = lax.dynamic_slice_in_dim(farmap, offset, slice_width, 3)
    weights_slice = lax.dynamic_slice_in_dim(weights, offset, slice_width, 0)
    adjoint_slice = cotangent_rows(fields_slice, farmap_slice, weights_slice)
    adjoint_blocks = gather_blocks(adjoint_slice, "dom", dom_size)
    adjoint = jnp.moveaxis(adjoint_blocks, 0, 1).reshape(2 * C, dir_count)
    stacked = stacked_rows(adjoint, vectors)
    coef_part, place_part = gradients(adjoint_terms(stacked, cos_tile, sin_tile), domain_rows)
    part = jnp.concatenate([coef_part, place_part], axis=0)
    reduced = scatter_sum(part, "dir", dir_size)
    return (reduced[: 2 * C].reshape(2, C, own_count), reduced[2 * C :])


def solution(mesh):
    placed = (
        P(None, None, ("dom", "dir")),
        P(None, ("dom", "dir")),
        P("dir"),
        P("dir"),
        P("dir"),
        P(None, None, None, "dir"),
    )
    return jax.shard_map(
        functools.partial(body, dir_size=mesh.shape["dir"], dom_size=mesh.shape["dom"]),
        mesh=mesh,
        in_specs=placed,
        out_specs=(P(None, None, ("dom", "dir")), P(None, ("dom", "dir"))),
        check_vma=False,
    )
```

```python
import functools

import jax
import jax.numpy as jnp
from jax import lax
from jax.sharding import PartitionSpec as P

C = 70


def unit_vectors(polar, azimuth):
    sine_polar = jnp.sin(polar)
    return jnp.stack([sine_polar * jnp.cos(azimuth), sine_polar * jnp.sin(azimuth), jnp.cos(polar)])


def phase_tile(places, vectors):
    angles = (
        places[0][:, None] * vectors[0][None, :]
        + places[1][:, None] * vectors[1][None, :]
        + places[2][:, None] * vectors[2][None, :]
    )
    return (jnp.cos(angles).astype(jnp.bfloat16), jnp.sin(angles).astype(jnp.bfloat16))


def field_terms(coef_block, cos_tile, sin_tile):
    order_count = coef_block.shape[0] // 2
    real_rows = coef_block[:order_count]
    imag_rows = coef_block[order_count:]
    top_rows = jnp.concatenate([real_rows, imag_rows], axis=1)
    low_rows = jnp.concatenate([imag_rows, -real_rows], axis=1)
    left_side = jnp.concatenate([top_rows, low_rows], axis=0)
    right_side = jnp.concatenate([cos_tile, sin_tile], axis=0)
    return jnp.dot(left_side, right_side, preferred_element_type=jnp.float32)


def adjoint_terms(stacked, cos_tile, sin_tile):
    order_count = stacked.shape[0] // 2
    real_rows = stacked[:order_count]
    imag_rows = stacked[order_count:]
    top_rows = jnp.concatenate([real_rows, imag_rows], axis=1)
    low_rows = jnp.concatenate([imag_rows, -real_rows], axis=1)
    left_side = jnp.concatenate([top_rows, low_rows], axis=0)
    right_side = jnp.concatenate([cos_tile, sin_tile], axis=1)
    return lax.dot_general(
        left_side, right_side, (((1,), (1,)), ((), ())), preferred_element_type=jnp.float32
    )


def amplitude_parts(fields, farmap):
    order_count = fields.shape[0] // 2
    field_real = fields[:order_count][None]
    field_imag = fields[order_count:][None]
    map_real = farmap[:, 0]
    map_imag = farmap[:, 1]
    amp_real = jnp.sum(map_real * field_real - map_imag * field_imag, axis=1)
    amp_imag = jnp.sum(map_real * field_imag + map_imag * field_real, axis=1)
    return (amp_real, amp_imag)


def cotangent_from(amp_real, amp_imag, farmap, weights):
    map_real = farmap[:, 0]
    map_imag = farmap[:, 1]
    cot_real = weights * jnp.sum(
        amp_real[:, None] * map_real + amp_imag[:, None] * map_imag, axis=0
    )
    cot_imag = weights * jnp.sum(
        amp_real[:, None] * map_imag - amp_imag[:, None] * map_real, axis=0
    )
    return jnp.concatenate([cot_real, cot_imag], axis=0).astype(jnp.bfloat16)


def cotangent_rows(fields, farmap, weights):
    amp_real, amp_imag = amplitude_parts(fields, farmap)
    return cotangent_from(amp_real, amp_imag, farmap, weights)


def stacked_rows(adjoint, vectors):
    order_count = adjoint.shape[0] // 2
    widened = adjoint.astype(jnp.float32)
    scaled = [(vectors[axis_id][None, :] * widened).astype(jnp.bfloat16) for axis_id in range(3)]
    real_parts = [adjoint[:order_count]] + [item[:order_count] for item in scaled]
    imag_parts = [adjoint[order_count:]] + [item[order_count:] for item in scaled]
    return jnp.concatenate(real_parts + imag_parts, axis=0)


def gradients(output, coef_block):
    order_count = coef_block.shape[0] // 2
    real_out = output[: 4 * order_count]
    imag_out = output[4 * order_count :]
    coef_term = jnp.concatenate(
        [2.0 * real_out[:order_count], -2.0 * imag_out[:order_count]], axis=0
    )
    coef_real = coef_block[:order_count].astype(jnp.float32)
    coef_imag = coef_block[order_count:].astype(jnp.float32)
    place_terms = []
    for axis_id in range(3):
        lower_row = (axis_id + 1) * order_count
        upper_row = (axis_id + 2) * order_count
        place_terms.append(
            2.0
            * jnp.sum(
                coef_real * imag_out[lower_row:upper_row]
                + coef_imag * real_out[lower_row:upper_row],
                axis=0,
            )
        )
    return (coef_term, jnp.stack(place_terms))


DOM_AXES = ("y", "z_lo", "core")
DIR_AXES = ("x", "z_hi")


def gather_blocks(block, axis_name, size):
    spread = jnp.broadcast_to(block[None], (size,) + block.shape)
    return lax.all_to_all(spread, axis_name, 0, 0, tiled=True)


def scatter_sum(part, axis_name, size):
    rows, width = part.shape
    split = part.reshape(rows, size, width // size)
    received = lax.all_to_all(split, axis_name, 1, 1, tiled=True)
    return jnp.sum(received, axis=1)


def gather_dir(block, sizes):
    inner = gather_blocks(block, DIR_AXES[1], sizes[1])
    outer = gather_blocks(inner, DIR_AXES[0], sizes[0])
    rows, width = block.shape
    return jnp.moveaxis(outer.reshape(sizes[0] * sizes[1], rows, width), 0, 1).reshape(
        rows, sizes[0] * sizes[1] * width
    )


def scatter_dir(part, sizes):
    rows, width = part.shape
    split = part.reshape(rows, sizes[0], sizes[1] * width // (sizes[0] * sizes[1]))
    outer = jnp.sum(lax.all_to_all(split, DIR_AXES[0], 1, 1, tiled=True), axis=1)
    return scatter_sum(outer, DIR_AXES[1], sizes[1])


def body(coefficients, positions, polar, azimuth, weights, farmap, dir_sizes, dom_size):
    own_count = coefficients.shape[2]
    own_rows = coefficients.reshape(2 * C, own_count)
    domain_rows = gather_dir(own_rows, dir_sizes)
    domain_places = gather_dir(positions, dir_sizes)
    vectors = unit_vectors(polar, azimuth)
    cos_tile, sin_tile = phase_tile(domain_places, vectors)
    partial_fields = field_terms(domain_rows, cos_tile, sin_tile)
    dir_count = polar.shape[0]
    slice_width = dir_count // dom_size
    fields_slice = scatter_sum(partial_fields, DOM_AXES, dom_size)
    offset = lax.axis_index(DOM_AXES) * slice_width
    farmap_slice = lax.dynamic_slice_in_dim(farmap, offset, slice_width, 3)
    weights_slice = lax.dynamic_slice_in_dim(weights, offset, slice_width, 0)
    adjoint_slice = cotangent_rows(fields_slice, farmap_slice, weights_slice)
    adjoint_blocks = gather_blocks(adjoint_slice, DOM_AXES, dom_size)
    adjoint = jnp.moveaxis(adjoint_blocks, 0, 1).reshape(2 * C, dir_count)
    stacked = stacked_rows(adjoint, vectors)
    coef_part, place_part = gradients(adjoint_terms(stacked, cos_tile, sin_tile), domain_rows)
    part = jnp.concatenate([coef_part, place_part], axis=0)
    reduced = scatter_dir(part, dir_sizes)
    return (reduced[: 2 * C].reshape(2, C, own_count), reduced[2 * C :])


def solution(mesh):
    dom_size = mesh.shape["dom"]
    dir_size = mesh.shape["dir"]
    chips_z = 2 if dom_size % 4 == 0 else 1
    dom_sizes = (dom_size // (2 * chips_z), chips_z, 2)
    x_size = 4 if dir_size % 4 == 0 else dir_size
    dir_sizes = (x_size, dir_size // x_size)
    fine = jax.sharding.Mesh(
        mesh.devices.reshape(dom_sizes + dir_sizes), DOM_AXES + DIR_AXES
    )
    every = DOM_AXES + DIR_AXES
    placed = (
        P(None, None, every),
        P(None, every),
        P(DIR_AXES),
        P(DIR_AXES),
        P(DIR_AXES),
        P(None, None, None, DIR_AXES),
    )
    return jax.shard_map(
        functools.partial(body, dir_sizes=dir_sizes, dom_size=dom_size),
        mesh=fine,
        in_specs=placed,
        out_specs=(P(None, None, every), P(None, every)),
        check_vma=False,
    )
```

```python
import functools

import jax
import jax.numpy as jnp
from jax import lax
from jax.sharding import PartitionSpec as P

C = 70


def unit_vectors(polar, azimuth):
    sine_polar = jnp.sin(polar)
    return jnp.stack([sine_polar * jnp.cos(azimuth), sine_polar * jnp.sin(azimuth), jnp.cos(polar)])


def phase_tile(places, vectors):
    angles = (
        places[0][:, None] * vectors[0][None, :]
        + places[1][:, None] * vectors[1][None, :]
        + places[2][:, None] * vectors[2][None, :]
    )
    return (jnp.cos(angles).astype(jnp.bfloat16), jnp.sin(angles).astype(jnp.bfloat16))


def field_terms(coef_block, cos_tile, sin_tile):
    order_count = coef_block.shape[0] // 2
    real_rows = coef_block[:order_count]
    imag_rows = coef_block[order_count:]
    top_rows = jnp.concatenate([real_rows, imag_rows], axis=1)
    low_rows = jnp.concatenate([imag_rows, -real_rows], axis=1)
    left_side = jnp.concatenate([top_rows, low_rows], axis=0)
    right_side = jnp.concatenate([cos_tile, sin_tile], axis=0)
    return jnp.dot(left_side, right_side, preferred_element_type=jnp.float32)


def adjoint_terms(stacked, cos_tile, sin_tile):
    order_count = stacked.shape[0] // 2
    real_rows = stacked[:order_count]
    imag_rows = stacked[order_count:]
    top_rows = jnp.concatenate([real_rows, imag_rows], axis=1)
    low_rows = jnp.concatenate([imag_rows, -real_rows], axis=1)
    left_side = jnp.concatenate([top_rows, low_rows], axis=0)
    right_side = jnp.concatenate([cos_tile, sin_tile], axis=1)
    return lax.dot_general(
        left_side, right_side, (((1,), (1,)), ((), ())), preferred_element_type=jnp.float32
    )


def amplitude_parts(fields, farmap):
    order_count = fields.shape[0] // 2
    field_real = fields[:order_count][None]
    field_imag = fields[order_count:][None]
    map_real = farmap[:, 0]
    map_imag = farmap[:, 1]
    amp_real = jnp.sum(map_real * field_real - map_imag * field_imag, axis=1)
    amp_imag = jnp.sum(map_real * field_imag + map_imag * field_real, axis=1)
    return (amp_real, amp_imag)


def cotangent_from(amp_real, amp_imag, farmap, weights):
    map_real = farmap[:, 0]
    map_imag = farmap[:, 1]
    cot_real = weights * jnp.sum(
        amp_real[:, None] * map_real + amp_imag[:, None] * map_imag, axis=0
    )
    cot_imag = weights * jnp.sum(
        amp_real[:, None] * map_imag - amp_imag[:, None] * map_real, axis=0
    )
    return jnp.concatenate([cot_real, cot_imag], axis=0).astype(jnp.bfloat16)


def cotangent_rows(fields, farmap, weights):
    amp_real, amp_imag = amplitude_parts(fields, farmap)
    return cotangent_from(amp_real, amp_imag, farmap, weights)


def stacked_rows(adjoint, vectors):
    order_count = adjoint.shape[0] // 2
    widened = adjoint.astype(jnp.float32)
    scaled = [(vectors[axis_id][None, :] * widened).astype(jnp.bfloat16) for axis_id in range(3)]
    real_parts = [adjoint[:order_count]] + [item[:order_count] for item in scaled]
    imag_parts = [adjoint[order_count:]] + [item[order_count:] for item in scaled]
    return jnp.concatenate(real_parts + imag_parts, axis=0)


def gradients(output, coef_block):
    order_count = coef_block.shape[0] // 2
    real_out = output[: 4 * order_count]
    imag_out = output[4 * order_count :]
    coef_term = jnp.concatenate(
        [2.0 * real_out[:order_count], -2.0 * imag_out[:order_count]], axis=0
    )
    coef_real = coef_block[:order_count].astype(jnp.float32)
    coef_imag = coef_block[order_count:].astype(jnp.float32)
    place_terms = []
    for axis_id in range(3):
        lower_row = (axis_id + 1) * order_count
        upper_row = (axis_id + 2) * order_count
        place_terms.append(
            2.0
            * jnp.sum(
                coef_real * imag_out[lower_row:upper_row]
                + coef_imag * real_out[lower_row:upper_row],
                axis=0,
            )
        )
    return (coef_term, jnp.stack(place_terms))


def gather_blocks(block, axis_name, size):
    spread = jnp.broadcast_to(block[None], (size,) + block.shape)
    return lax.all_to_all(spread, axis_name, 0, 0, tiled=True)


def scatter_sum(part, axis_name, size):
    rows, width = part.shape
    split = part.reshape(rows, size, width // size)
    received = lax.all_to_all(split, axis_name, 1, 1, tiled=True)
    return jnp.sum(received, axis=1)


def body(coefficients, positions, polar, azimuth, weights, farmap, dir_size, dom_size):
    own_count = coefficients.shape[2]
    own_rows = coefficients.reshape(2 * C, own_count)
    coef_blocks = gather_blocks(own_rows, "dom", dom_size)
    place_blocks = gather_blocks(positions, "dom", dom_size)
    domain_rows = jnp.moveaxis(coef_blocks, 0, 1).reshape(2 * C, dom_size * own_count)
    domain_places = jnp.moveaxis(place_blocks, 0, 1).reshape(3, dom_size * own_count)
    slice_width = polar.shape[0] // dom_size
    offset = lax.axis_index("dom") * slice_width
    own_angles = lax.dynamic_slice_in_dim(jnp.stack([polar, azimuth]), offset, slice_width, 1)
    angle_blocks = gather_blocks(own_angles, "dir", dir_size)
    set_angles = jnp.moveaxis(angle_blocks, 0, 1).reshape(2, dir_size * slice_width)
    vectors = unit_vectors(set_angles[0], set_angles[1])
    cos_tile, sin_tile = phase_tile(domain_places, vectors)
    partial_fields = field_terms(domain_rows, cos_tile, sin_tile)
    fields_slice = scatter_sum(partial_fields, "dir", dir_size)
    farmap_slice = lax.dynamic_slice_in_dim(farmap, offset, slice_width, 3)
    weights_slice = lax.dynamic_slice_in_dim(weights, offset, slice_width, 0)
    adjoint_slice = cotangent_rows(fields_slice, farmap_slice, weights_slice)
    adjoint_blocks = gather_blocks(adjoint_slice, "dir", dir_size)
    adjoint = jnp.moveaxis(adjoint_blocks, 0, 1).reshape(2 * C, dir_size * slice_width)
    stacked = stacked_rows(adjoint, vectors)
    coef_part, place_part = gradients(adjoint_terms(stacked, cos_tile, sin_tile), domain_rows)
    part = jnp.concatenate([coef_part, place_part], axis=0)
    reduced = scatter_sum(part, "dom", dom_size)
    return (reduced[: 2 * C].reshape(2, C, own_count), reduced[2 * C :])


def solution(mesh):
    placed = (
        P(None, None, ("dom", "dir")),
        P(None, ("dom", "dir")),
        P("dir"),
        P("dir"),
        P("dir"),
        P(None, None, None, "dir"),
    )
    return jax.shard_map(
        functools.partial(body, dir_size=mesh.shape["dir"], dom_size=mesh.shape["dom"]),
        mesh=mesh,
        in_specs=placed,
        out_specs=(P(None, None, ("dom", "dir")), P(None, ("dom", "dir"))),
        check_vma=False,
    )
```

```python
import functools

import jax
import jax.numpy as jnp
from jax import lax
from jax.sharding import PartitionSpec as P

C = 70


def unit_vectors(polar, azimuth):
    sine_polar = jnp.sin(polar)
    return jnp.stack([sine_polar * jnp.cos(azimuth), sine_polar * jnp.sin(azimuth), jnp.cos(polar)])


def phase_tile(places, vectors):
    angles = (
        places[0][:, None] * vectors[0][None, :]
        + places[1][:, None] * vectors[1][None, :]
        + places[2][:, None] * vectors[2][None, :]
    )
    return (jnp.cos(angles).astype(jnp.bfloat16), jnp.sin(angles).astype(jnp.bfloat16))


def field_terms(coef_block, cos_tile, sin_tile):
    order_count = coef_block.shape[0] // 2
    real_rows = coef_block[:order_count]
    imag_rows = coef_block[order_count:]
    top_rows = jnp.concatenate([real_rows, imag_rows], axis=1)
    low_rows = jnp.concatenate([imag_rows, -real_rows], axis=1)
    left_side = jnp.concatenate([top_rows, low_rows], axis=0)
    right_side = jnp.concatenate([cos_tile, sin_tile], axis=0)
    return jnp.dot(left_side, right_side, preferred_element_type=jnp.float32)


def adjoint_terms(stacked, cos_tile, sin_tile):
    order_count = stacked.shape[0] // 2
    real_rows = stacked[:order_count]
    imag_rows = stacked[order_count:]
    top_rows = jnp.concatenate([real_rows, imag_rows], axis=1)
    low_rows = jnp.concatenate([imag_rows, -real_rows], axis=1)
    left_side = jnp.concatenate([top_rows, low_rows], axis=0)
    right_side = jnp.concatenate([cos_tile, sin_tile], axis=1)
    return lax.dot_general(
        left_side, right_side, (((1,), (1,)), ((), ())), preferred_element_type=jnp.float32
    )


def amplitude_parts(fields, farmap):
    order_count = fields.shape[0] // 2
    field_real = fields[:order_count][None]
    field_imag = fields[order_count:][None]
    map_real = farmap[:, 0]
    map_imag = farmap[:, 1]
    amp_real = jnp.sum(map_real * field_real - map_imag * field_imag, axis=1)
    amp_imag = jnp.sum(map_real * field_imag + map_imag * field_real, axis=1)
    return (amp_real, amp_imag)


def cotangent_from(amp_real, amp_imag, farmap, weights):
    map_real = farmap[:, 0]
    map_imag = farmap[:, 1]
    cot_real = weights * jnp.sum(
        amp_real[:, None] * map_real + amp_imag[:, None] * map_imag, axis=0
    )
    cot_imag = weights * jnp.sum(
        amp_real[:, None] * map_imag - amp_imag[:, None] * map_real, axis=0
    )
    return jnp.concatenate([cot_real, cot_imag], axis=0).astype(jnp.bfloat16)


def cotangent_rows(fields, farmap, weights):
    amp_real, amp_imag = amplitude_parts(fields, farmap)
    return cotangent_from(amp_real, amp_imag, farmap, weights)


def stacked_rows(adjoint, vectors):
    order_count = adjoint.shape[0] // 2
    widened = adjoint.astype(jnp.float32)
    scaled = [(vectors[axis_id][None, :] * widened).astype(jnp.bfloat16) for axis_id in range(3)]
    real_parts = [adjoint[:order_count]] + [item[:order_count] for item in scaled]
    imag_parts = [adjoint[order_count:]] + [item[order_count:] for item in scaled]
    return jnp.concatenate(real_parts + imag_parts, axis=0)


def gradients(output, coef_block):
    order_count = coef_block.shape[0] // 2
    real_out = output[: 4 * order_count]
    imag_out = output[4 * order_count :]
    coef_term = jnp.concatenate(
        [2.0 * real_out[:order_count], -2.0 * imag_out[:order_count]], axis=0
    )
    coef_real = coef_block[:order_count].astype(jnp.float32)
    coef_imag = coef_block[order_count:].astype(jnp.float32)
    place_terms = []
    for axis_id in range(3):
        lower_row = (axis_id + 1) * order_count
        upper_row = (axis_id + 2) * order_count
        place_terms.append(
            2.0
            * jnp.sum(
                coef_real * imag_out[lower_row:upper_row]
                + coef_imag * real_out[lower_row:upper_row],
                axis=0,
            )
        )
    return (coef_term, jnp.stack(place_terms))


DOM_AXES = ("y", "z_lo", "core")
DIR_AXES = ("x", "z_hi")


def gather_blocks(block, axis_name, size):
    spread = jnp.broadcast_to(block[None], (size,) + block.shape)
    return lax.all_to_all(spread, axis_name, 0, 0, tiled=True)


def scatter_sum(part, axis_name, size):
    rows, width = part.shape
    split = part.reshape(rows, size, width // size)
    received = lax.all_to_all(split, axis_name, 1, 1, tiled=True)
    return jnp.sum(received, axis=1)


def scatter_dir(part, sizes):
    rows, width = part.shape
    split = part.reshape(rows, sizes[0], sizes[1] * width // (sizes[0] * sizes[1]))
    outer = jnp.sum(lax.all_to_all(split, DIR_AXES[0], 1, 1, tiled=True), axis=1)
    return scatter_sum(outer, DIR_AXES[1], sizes[1])


def body(coefficients, positions, polar, azimuth, weights, farmap, dir_sizes, dom_size):
    own_count = coefficients.shape[2]
    dir_size = dir_sizes[0] * dir_sizes[1]
    own_rows = coefficients.reshape(2 * C, own_count)
    place_blocks = gather_blocks(positions, DIR_AXES, dir_size)
    domain_places = jnp.moveaxis(place_blocks, 0, 1).reshape(3, dir_size * own_count)
    own_rows, domain_places = lax.optimization_barrier((own_rows, domain_places))
    coef_blocks = gather_blocks(own_rows, DIR_AXES, dir_size)
    domain_rows = jnp.moveaxis(coef_blocks, 0, 1).reshape(2 * C, dir_size * own_count)
    vectors = unit_vectors(polar, azimuth)
    cos_tile, sin_tile = phase_tile(domain_places, vectors)
    partial_fields = field_terms(domain_rows, cos_tile, sin_tile)
    dir_count = polar.shape[0]
    slice_width = dir_count // dom_size
    fields_slice = scatter_sum(partial_fields, DOM_AXES, dom_size)
    offset = lax.axis_index(DOM_AXES) * slice_width
    farmap_slice = lax.dynamic_slice_in_dim(farmap, offset, slice_width, 3)
    weights_slice = lax.dynamic_slice_in_dim(weights, offset, slice_width, 0)
    adjoint_slice = cotangent_rows(fields_slice, farmap_slice, weights_slice)
    adjoint_blocks = gather_blocks(adjoint_slice, DOM_AXES, dom_size)
    adjoint = jnp.moveaxis(adjoint_blocks, 0, 1).reshape(2 * C, dir_count)
    stacked = stacked_rows(adjoint, vectors)
    coef_part, place_part = gradients(adjoint_terms(stacked, cos_tile, sin_tile), domain_rows)
    part = jnp.concatenate([coef_part, place_part], axis=0)
    reduced = scatter_dir(part, dir_sizes)
    return (reduced[: 2 * C].reshape(2, C, own_count), reduced[2 * C :])


def solution(mesh):
    dom_size = mesh.shape["dom"]
    dir_size = mesh.shape["dir"]
    chips_z = 2 if dom_size % 4 == 0 else 1
    dom_sizes = (dom_size // (2 * chips_z), chips_z, 2)
    x_size = 4 if dir_size % 4 == 0 else dir_size
    dir_sizes = (x_size, dir_size // x_size)
    fine = jax.sharding.Mesh(
        mesh.devices.reshape(dom_sizes + dir_sizes), DOM_AXES + DIR_AXES
    )
    every = DOM_AXES + DIR_AXES
    placed = (
        P(None, None, every),
        P(None, every),
        P(DIR_AXES),
        P(DIR_AXES),
        P(DIR_AXES),
        P(None, None, None, DIR_AXES),
    )
    return jax.shard_map(
        functools.partial(body, dir_sizes=dir_sizes, dom_size=dom_size),
        mesh=fine,
        in_specs=placed,
        out_specs=(P(None, None, every), P(None, every)),
        check_vma=False,
    )
```

```python
import functools

import jax
import jax.numpy as jnp
from jax import lax
from jax.sharding import PartitionSpec as P

C = 70


def unit_vectors(polar, azimuth):
    sine_polar = jnp.sin(polar)
    return jnp.stack([sine_polar * jnp.cos(azimuth), sine_polar * jnp.sin(azimuth), jnp.cos(polar)])


def phase_tile(places, vectors):
    angles = (
        places[0][:, None] * vectors[0][None, :]
        + places[1][:, None] * vectors[1][None, :]
        + places[2][:, None] * vectors[2][None, :]
    )
    return (jnp.cos(angles).astype(jnp.bfloat16), jnp.sin(angles).astype(jnp.bfloat16))


def field_terms(coef_block, cos_tile, sin_tile):
    order_count = coef_block.shape[0] // 2
    real_rows = coef_block[:order_count]
    imag_rows = coef_block[order_count:]
    top_rows = jnp.concatenate([real_rows, imag_rows], axis=1)
    low_rows = jnp.concatenate([imag_rows, -real_rows], axis=1)
    left_side = jnp.concatenate([top_rows, low_rows], axis=0)
    right_side = jnp.concatenate([cos_tile, sin_tile], axis=0)
    return jnp.dot(left_side, right_side, preferred_element_type=jnp.float32)


def adjoint_terms(stacked, cos_tile, sin_tile):
    order_count = stacked.shape[0] // 2
    real_rows = stacked[:order_count]
    imag_rows = stacked[order_count:]
    top_rows = jnp.concatenate([real_rows, imag_rows], axis=1)
    low_rows = jnp.concatenate([imag_rows, -real_rows], axis=1)
    left_side = jnp.concatenate([top_rows, low_rows], axis=0)
    right_side = jnp.concatenate([cos_tile, sin_tile], axis=1)
    return lax.dot_general(
        left_side, right_side, (((1,), (1,)), ((), ())), preferred_element_type=jnp.float32
    )


def amplitude_parts(fields, farmap):
    order_count = fields.shape[0] // 2
    field_real = fields[:order_count][None]
    field_imag = fields[order_count:][None]
    map_real = farmap[:, 0]
    map_imag = farmap[:, 1]
    amp_real = jnp.sum(map_real * field_real - map_imag * field_imag, axis=1)
    amp_imag = jnp.sum(map_real * field_imag + map_imag * field_real, axis=1)
    return (amp_real, amp_imag)


def cotangent_from(amp_real, amp_imag, farmap, weights):
    map_real = farmap[:, 0]
    map_imag = farmap[:, 1]
    cot_real = weights * jnp.sum(
        amp_real[:, None] * map_real + amp_imag[:, None] * map_imag, axis=0
    )
    cot_imag = weights * jnp.sum(
        amp_real[:, None] * map_imag - amp_imag[:, None] * map_real, axis=0
    )
    return jnp.concatenate([cot_real, cot_imag], axis=0).astype(jnp.bfloat16)


def cotangent_rows(fields, farmap, weights):
    amp_real, amp_imag = amplitude_parts(fields, farmap)
    return cotangent_from(amp_real, amp_imag, farmap, weights)


def stacked_rows(adjoint, vectors):
    order_count = adjoint.shape[0] // 2
    widened = adjoint.astype(jnp.float32)
    scaled = [(vectors[axis_id][None, :] * widened).astype(jnp.bfloat16) for axis_id in range(3)]
    real_parts = [adjoint[:order_count]] + [item[:order_count] for item in scaled]
    imag_parts = [adjoint[order_count:]] + [item[order_count:] for item in scaled]
    return jnp.concatenate(real_parts + imag_parts, axis=0)


def gradients(output, coef_block):
    order_count = coef_block.shape[0] // 2
    real_out = output[: 4 * order_count]
    imag_out = output[4 * order_count :]
    coef_term = jnp.concatenate(
        [2.0 * real_out[:order_count], -2.0 * imag_out[:order_count]], axis=0
    )
    coef_real = coef_block[:order_count].astype(jnp.float32)
    coef_imag = coef_block[order_count:].astype(jnp.float32)
    place_terms = []
    for axis_id in range(3):
        lower_row = (axis_id + 1) * order_count
        upper_row = (axis_id + 2) * order_count
        place_terms.append(
            2.0
            * jnp.sum(
                coef_real * imag_out[lower_row:upper_row]
                + coef_imag * real_out[lower_row:upper_row],
                axis=0,
            )
        )
    return (coef_term, jnp.stack(place_terms))


DOM_AXES = ("y", "z_lo", "core")
DIR_AXES = ("x", "z_hi")


def gather_blocks(block, axis_name, size):
    spread = jnp.broadcast_to(block[None], (size,) + block.shape)
    return lax.all_to_all(spread, axis_name, 0, 0, tiled=True)


def scatter_sum(part, axis_name, size):
    rows, width = part.shape
    split = part.reshape(rows, size, width // size)
    received = lax.all_to_all(split, axis_name, 1, 1, tiled=True)
    return jnp.sum(received, axis=1)


def scatter_dir(part, sizes):
    rows, width = part.shape
    split = part.reshape(rows, sizes[0], sizes[1] * width // (sizes[0] * sizes[1]))
    received = lax.all_to_all(narrow_rows(split), DIR_AXES[0], 1, 1, tiled=True)
    outer = jnp.sum(widen_rows(received), axis=1)
    inner = outer.reshape(rows, sizes[1], width // (sizes[0] * sizes[1]))
    received = lax.all_to_all(narrow_rows(inner), DIR_AXES[1], 1, 1, tiled=True)
    return jnp.sum(widen_rows(received), axis=1)


def narrow_rows(part):
    coef_rows = part[: 2 * C].astype(jnp.bfloat16)
    place_high = part[2 * C :].astype(jnp.bfloat16)
    place_low = (part[2 * C :] - place_high.astype(jnp.float32)).astype(jnp.bfloat16)
    return jnp.concatenate([coef_rows, place_high, place_low], axis=0)


def widen_rows(packed):
    wide = packed.astype(jnp.float32)
    place_count = (packed.shape[0] - 2 * C) // 2
    place_rows = wide[2 * C : 2 * C + place_count] + wide[2 * C + place_count :]
    return jnp.concatenate([wide[: 2 * C], place_rows], axis=0)


def body(coefficients, positions, polar, azimuth, weights, farmap, dir_sizes, dom_size):
    own_count = coefficients.shape[2]
    dir_size = dir_sizes[0] * dir_sizes[1]
    own_rows = coefficients.reshape(2 * C, own_count)
    place_blocks = gather_blocks(positions, DIR_AXES, dir_size)
    domain_places = jnp.moveaxis(place_blocks, 0, 1).reshape(3, dir_size * own_count)
    own_rows, domain_places = lax.optimization_barrier((own_rows, domain_places))
    coef_blocks = gather_blocks(own_rows, DIR_AXES, dir_size)
    domain_rows = jnp.moveaxis(coef_blocks, 0, 1).reshape(2 * C, dir_size * own_count)
    vectors = unit_vectors(polar, azimuth)
    cos_tile, sin_tile = phase_tile(domain_places, vectors)
    partial_fields = field_terms(domain_rows, cos_tile, sin_tile)
    dir_count = polar.shape[0]
    slice_width = dir_count // dom_size
    fields_slice = scatter_sum(partial_fields, DOM_AXES, dom_size)
    offset = lax.axis_index(DOM_AXES) * slice_width
    farmap_slice = lax.dynamic_slice_in_dim(farmap, offset, slice_width, 3)
    weights_slice = lax.dynamic_slice_in_dim(weights, offset, slice_width, 0)
    adjoint_slice = cotangent_rows(fields_slice, farmap_slice, weights_slice)
    adjoint_blocks = gather_blocks(adjoint_slice, DOM_AXES, dom_size)
    adjoint = jnp.moveaxis(adjoint_blocks, 0, 1).reshape(2 * C, dir_count)
    stacked = stacked_rows(adjoint, vectors)
    coef_part, place_part = gradients(adjoint_terms(stacked, cos_tile, sin_tile), domain_rows)
    part = jnp.concatenate([coef_part, place_part], axis=0)
    reduced = scatter_dir(part, dir_sizes)
    return (reduced[: 2 * C].reshape(2, C, own_count), reduced[2 * C :])


def solution(mesh):
    dom_size = mesh.shape["dom"]
    dir_size = mesh.shape["dir"]
    chips_z = 2 if dom_size % 4 == 0 else 1
    dom_sizes = (dom_size // (2 * chips_z), chips_z, 2)
    x_size = 4 if dir_size % 4 == 0 else dir_size
    dir_sizes = (x_size, dir_size // x_size)
    fine = jax.sharding.Mesh(
        mesh.devices.reshape(dom_sizes + dir_sizes), DOM_AXES + DIR_AXES
    )
    every = DOM_AXES + DIR_AXES
    placed = (
        P(None, None, every),
        P(None, every),
        P(DIR_AXES),
        P(DIR_AXES),
        P(DIR_AXES),
        P(None, None, None, DIR_AXES),
    )
    return jax.shard_map(
        functools.partial(body, dir_sizes=dir_sizes, dom_size=dom_size),
        mesh=fine,
        in_specs=placed,
        out_specs=(P(None, None, every), P(None, every)),
        check_vma=False,
    )
```

```python
import functools

import jax
import jax.numpy as jnp
from jax import lax
from jax.sharding import PartitionSpec as P

C = 70


def unit_vectors(polar, azimuth):
    sine_polar = jnp.sin(polar)
    return jnp.stack([sine_polar * jnp.cos(azimuth), sine_polar * jnp.sin(azimuth), jnp.cos(polar)])


def phase_tile(places, vectors):
    angles = (
        places[0][:, None] * vectors[0][None, :]
        + places[1][:, None] * vectors[1][None, :]
        + places[2][:, None] * vectors[2][None, :]
    )
    return (jnp.cos(angles).astype(jnp.bfloat16), jnp.sin(angles).astype(jnp.bfloat16))


def field_terms(coef_block, cos_tile, sin_tile):
    order_count = coef_block.shape[0] // 2
    real_rows = coef_block[:order_count]
    imag_rows = coef_block[order_count:]
    top_rows = jnp.concatenate([real_rows, imag_rows], axis=1)
    low_rows = jnp.concatenate([imag_rows, -real_rows], axis=1)
    left_side = jnp.concatenate([top_rows, low_rows], axis=0)
    right_side = jnp.concatenate([cos_tile, sin_tile], axis=0)
    return jnp.dot(left_side, right_side, preferred_element_type=jnp.float32)


def adjoint_terms(stacked, cos_tile, sin_tile):
    order_count = stacked.shape[0] // 2
    real_rows = stacked[:order_count]
    imag_rows = stacked[order_count:]
    top_rows = jnp.concatenate([real_rows, imag_rows], axis=1)
    low_rows = jnp.concatenate([imag_rows, -real_rows], axis=1)
    left_side = jnp.concatenate([top_rows, low_rows], axis=0)
    right_side = jnp.concatenate([cos_tile, sin_tile], axis=1)
    return lax.dot_general(
        left_side, right_side, (((1,), (1,)), ((), ())), preferred_element_type=jnp.float32
    )


def amplitude_parts(fields, farmap):
    order_count = fields.shape[0] // 2
    field_real = fields[:order_count][None]
    field_imag = fields[order_count:][None]
    map_real = farmap[:, 0]
    map_imag = farmap[:, 1]
    amp_real = jnp.sum(map_real * field_real - map_imag * field_imag, axis=1)
    amp_imag = jnp.sum(map_real * field_imag + map_imag * field_real, axis=1)
    return (amp_real, amp_imag)


def cotangent_from(amp_real, amp_imag, farmap, weights):
    map_real = farmap[:, 0]
    map_imag = farmap[:, 1]
    cot_real = weights * jnp.sum(
        amp_real[:, None] * map_real + amp_imag[:, None] * map_imag, axis=0
    )
    cot_imag = weights * jnp.sum(
        amp_real[:, None] * map_imag - amp_imag[:, None] * map_real, axis=0
    )
    return jnp.concatenate([cot_real, cot_imag], axis=0).astype(jnp.bfloat16)


def cotangent_rows(fields, farmap, weights):
    amp_real, amp_imag = amplitude_parts(fields, farmap)
    return cotangent_from(amp_real, amp_imag, farmap, weights)


def stacked_rows(adjoint, vectors):
    order_count = adjoint.shape[0] // 2
    widened = adjoint.astype(jnp.float32)
    scaled = [(vectors[axis_id][None, :] * widened).astype(jnp.bfloat16) for axis_id in range(3)]
    real_parts = [adjoint[:order_count]] + [item[:order_count] for item in scaled]
    imag_parts = [adjoint[order_count:]] + [item[order_count:] for item in scaled]
    return jnp.concatenate(real_parts + imag_parts, axis=0)


def gradients(output, coef_block):
    order_count = coef_block.shape[0] // 2
    real_out = output[: 4 * order_count]
    imag_out = output[4 * order_count :]
    coef_term = jnp.concatenate(
        [2.0 * real_out[:order_count], -2.0 * imag_out[:order_count]], axis=0
    )
    coef_real = coef_block[:order_count].astype(jnp.float32)
    coef_imag = coef_block[order_count:].astype(jnp.float32)
    place_terms = []
    for axis_id in range(3):
        lower_row = (axis_id + 1) * order_count
        upper_row = (axis_id + 2) * order_count
        place_terms.append(
            2.0
            * jnp.sum(
                coef_real * imag_out[lower_row:upper_row]
                + coef_imag * real_out[lower_row:upper_row],
                axis=0,
            )
        )
    return (coef_term, jnp.stack(place_terms))


DOM_AXES = ("y", "z_lo", "core")
DIR_AXES = ("x", "z_hi")


def gather_blocks(block, axis_name, size):
    spread = jnp.broadcast_to(block[None], (size,) + block.shape)
    return lax.all_to_all(spread, axis_name, 0, 0, tiled=True)


def scatter_sum(part, axis_name, size):
    rows, width = part.shape
    split = part.reshape(rows, size, width // size)
    received = lax.all_to_all(split, axis_name, 1, 1, tiled=True)
    return jnp.sum(received, axis=1)


def scatter_dir(part, sizes):
    rows, width = part.shape
    size = sizes[0] * sizes[1]
    split = part.reshape(rows, size, width // size)
    received = lax.all_to_all(narrow_rows(split), DIR_AXES, 1, 1, tiled=True)
    return jnp.sum(widen_rows(received), axis=1)


def narrow_rows(part):
    coef_rows = part[: 2 * C].astype(jnp.bfloat16)
    place_high = part[2 * C :].astype(jnp.bfloat16)
    place_low = (part[2 * C :] - place_high.astype(jnp.float32)).astype(jnp.bfloat16)
    return jnp.concatenate([coef_rows, place_high, place_low], axis=0)


def widen_rows(packed):
    wide = packed.astype(jnp.float32)
    place_count = (packed.shape[0] - 2 * C) // 2
    place_rows = wide[2 * C : 2 * C + place_count] + wide[2 * C + place_count :]
    return jnp.concatenate([wide[: 2 * C], place_rows], axis=0)


def body(coefficients, positions, polar, azimuth, weights, farmap, dir_sizes, dom_size):
    own_count = coefficients.shape[2]
    dir_size = dir_sizes[0] * dir_sizes[1]
    own_rows = coefficients.reshape(2 * C, own_count)
    place_blocks = gather_blocks(positions, DIR_AXES, dir_size)
    domain_places = jnp.moveaxis(place_blocks, 0, 1).reshape(3, dir_size * own_count)
    own_rows, domain_places = lax.optimization_barrier((own_rows, domain_places))
    coef_blocks = gather_blocks(own_rows, DIR_AXES, dir_size)
    domain_rows = jnp.moveaxis(coef_blocks, 0, 1).reshape(2 * C, dir_size * own_count)
    vectors = unit_vectors(polar, azimuth)
    cos_tile, sin_tile = phase_tile(domain_places, vectors)
    partial_fields = field_terms(domain_rows, cos_tile, sin_tile)
    dir_count = polar.shape[0]
    slice_width = dir_count // dom_size
    fields_slice = scatter_sum(partial_fields, DOM_AXES, dom_size)
    offset = lax.axis_index(DOM_AXES) * slice_width
    farmap_slice = lax.dynamic_slice_in_dim(farmap, offset, slice_width, 3)
    weights_slice = lax.dynamic_slice_in_dim(weights, offset, slice_width, 0)
    adjoint_slice = cotangent_rows(fields_slice, farmap_slice, weights_slice)
    adjoint_blocks = gather_blocks(adjoint_slice, DOM_AXES, dom_size)
    adjoint = jnp.moveaxis(adjoint_blocks, 0, 1).reshape(2 * C, dir_count)
    stacked = stacked_rows(adjoint, vectors)
    coef_part, place_part = gradients(adjoint_terms(stacked, cos_tile, sin_tile), domain_rows)
    part = jnp.concatenate([coef_part, place_part], axis=0)
    reduced = scatter_dir(part, dir_sizes)
    return (reduced[: 2 * C].reshape(2, C, own_count), reduced[2 * C :])


def solution(mesh):
    dom_size = mesh.shape["dom"]
    dir_size = mesh.shape["dir"]
    chips_z = 2 if dom_size % 4 == 0 else 1
    dom_sizes = (dom_size // (2 * chips_z), chips_z, 2)
    x_size = 4 if dir_size % 4 == 0 else dir_size
    dir_sizes = (x_size, dir_size // x_size)
    fine = jax.sharding.Mesh(
        mesh.devices.reshape(dom_sizes + dir_sizes), DOM_AXES + DIR_AXES
    )
    every = DOM_AXES + DIR_AXES
    placed = (
        P(None, None, every),
        P(None, every),
        P(DIR_AXES),
        P(DIR_AXES),
        P(DIR_AXES),
        P(None, None, None, DIR_AXES),
    )
    return jax.shard_map(
        functools.partial(body, dir_sizes=dir_sizes, dom_size=dom_size),
        mesh=fine,
        in_specs=placed,
        out_specs=(P(None, None, every), P(None, every)),
        check_vma=False,
    )
```

```python
import functools

import jax
import jax.numpy as jnp
from jax import lax
import numpy as np
from jax.sharding import PartitionSpec as P

C = 70


def unit_vectors(polar, azimuth):
    sine_polar = jnp.sin(polar)
    return jnp.stack([sine_polar * jnp.cos(azimuth), sine_polar * jnp.sin(azimuth), jnp.cos(polar)])


def sine_cosine(angles):
    quarter = jnp.round(angles * np.float32(2.0 / np.pi))
    reduced = angles - quarter * np.float32(1.5703125)
    reduced = reduced - quarter * np.float32(4.837512969970703125e-4)
    reduced = reduced - quarter * np.float32(7.54978995489188216e-8)
    square = reduced * reduced
    sine = reduced + reduced * square * (
        np.float32(-1 / 6)
        + square * (np.float32(1 / 120) + square * (np.float32(-1 / 5040) + square * np.float32(1 / 362880)))
    )
    cosine = np.float32(1) + square * (
        np.float32(-0.5)
        + square * (np.float32(1 / 24) + square * (np.float32(-1 / 720) + square * np.float32(1 / 40320)))
    )
    turn = quarter.astype(jnp.int32)
    odd = (turn & 1) == 1
    cos_base = jnp.where(odd, sine, cosine)
    sin_base = jnp.where(odd, cosine, sine)
    cos_value = jnp.where(((turn + 1) & 2) == 2, -cos_base, cos_base)
    sin_value = jnp.where((turn & 2) == 2, -sin_base, sin_base)
    return (cos_value, sin_value)


def phase_tile(places, vectors):
    angles = (
        places[0][:, None] * vectors[0][None, :]
        + places[1][:, None] * vectors[1][None, :]
        + places[2][:, None] * vectors[2][None, :]
    )
    cos_value, sin_value = sine_cosine(angles)
    return (cos_value.astype(jnp.bfloat16), sin_value.astype(jnp.bfloat16))


def field_terms(coef_block, cos_tile, sin_tile):
    order_count = coef_block.shape[0] // 2
    real_rows = coef_block[:order_count]
    imag_rows = coef_block[order_count:]
    top_rows = jnp.concatenate([real_rows, imag_rows], axis=1)
    low_rows = jnp.concatenate([imag_rows, -real_rows], axis=1)
    left_side = jnp.concatenate([top_rows, low_rows], axis=0)
    right_side = jnp.concatenate([cos_tile, sin_tile], axis=0)
    return jnp.dot(left_side, right_side, preferred_element_type=jnp.float32)


def adjoint_terms(stacked, cos_tile, sin_tile):
    order_count = stacked.shape[0] // 2
    real_rows = stacked[:order_count]
    imag_rows = stacked[order_count:]
    top_rows = jnp.concatenate([real_rows, imag_rows], axis=1)
    low_rows = jnp.concatenate([imag_rows, -real_rows], axis=1)
    left_side = jnp.concatenate([top_rows, low_rows], axis=0)
    right_side = jnp.concatenate([cos_tile, sin_tile], axis=1)
    return lax.dot_general(
        left_side, right_side, (((1,), (1,)), ((), ())), preferred_element_type=jnp.float32
    )


def amplitude_parts(fields, farmap):
    order_count = fields.shape[0] // 2
    field_real = fields[:order_count][None]
    field_imag = fields[order_count:][None]
    map_real = farmap[:, 0]
    map_imag = farmap[:, 1]
    amp_real = jnp.sum(map_real * field_real - map_imag * field_imag, axis=1)
    amp_imag = jnp.sum(map_real * field_imag + map_imag * field_real, axis=1)
    return (amp_real, amp_imag)


def cotangent_from(amp_real, amp_imag, farmap, weights):
    map_real = farmap[:, 0]
    map_imag = farmap[:, 1]
    cot_real = weights * jnp.sum(
        amp_real[:, None] * map_real + amp_imag[:, None] * map_imag, axis=0
    )
    cot_imag = weights * jnp.sum(
        amp_real[:, None] * map_imag - amp_imag[:, None] * map_real, axis=0
    )
    return jnp.concatenate([cot_real, cot_imag], axis=0).astype(jnp.bfloat16)


def cotangent_rows(fields, farmap, weights):
    amp_real, amp_imag = amplitude_parts(fields, farmap)
    return cotangent_from(amp_real, amp_imag, farmap, weights)


def stacked_rows(adjoint, vectors):
    order_count = adjoint.shape[0] // 2
    widened = adjoint.astype(jnp.float32)
    scaled = [(vectors[axis_id][None, :] * widened).astype(jnp.bfloat16) for axis_id in range(3)]
    real_parts = [adjoint[:order_count]] + [item[:order_count] for item in scaled]
    imag_parts = [adjoint[order_count:]] + [item[order_count:] for item in scaled]
    return jnp.concatenate(real_parts + imag_parts, axis=0)


def gradients(output, coef_block):
    order_count = coef_block.shape[0] // 2
    real_out = output[: 4 * order_count]
    imag_out = output[4 * order_count :]
    coef_term = jnp.concatenate(
        [2.0 * real_out[:order_count], -2.0 * imag_out[:order_count]], axis=0
    )
    coef_real = coef_block[:order_count].astype(jnp.float32)
    coef_imag = coef_block[order_count:].astype(jnp.float32)
    place_terms = []
    for axis_id in range(3):
        lower_row = (axis_id + 1) * order_count
        upper_row = (axis_id + 2) * order_count
        place_terms.append(
            2.0
            * jnp.sum(
                coef_real * imag_out[lower_row:upper_row]
                + coef_imag * real_out[lower_row:upper_row],
                axis=0,
            )
        )
    return (coef_term, jnp.stack(place_terms))


DOM_AXES = ("y", "z_lo", "core")
DIR_AXES = ("x", "z_hi")


def gather_blocks(block, axis_name, size):
    spread = jnp.broadcast_to(block[None], (size,) + block.shape)
    return lax.all_to_all(spread, axis_name, 0, 0, tiled=True)


def scatter_sum(part, axis_name, size):
    rows, width = part.shape
    split = part.reshape(rows, size, width // size)
    received = lax.all_to_all(split, axis_name, 1, 1, tiled=True)
    return jnp.sum(received, axis=1)


def scatter_dir(part, sizes):
    rows, width = part.shape
    size = sizes[0] * sizes[1]
    split = part.reshape(rows, size, width // size)
    received = lax.all_to_all(narrow_rows(split), DIR_AXES, 1, 1, tiled=True)
    return jnp.sum(widen_rows(received), axis=1)


def narrow_rows(part):
    coef_rows = part[: 2 * C].astype(jnp.bfloat16)
    place_high = part[2 * C :].astype(jnp.bfloat16)
    place_low = (part[2 * C :] - place_high.astype(jnp.float32)).astype(jnp.bfloat16)
    return jnp.concatenate([coef_rows, place_high, place_low], axis=0)


def widen_rows(packed):
    wide = packed.astype(jnp.float32)
    place_count = (packed.shape[0] - 2 * C) // 2
    place_rows = wide[2 * C : 2 * C + place_count] + wide[2 * C + place_count :]
    return jnp.concatenate([wide[: 2 * C], place_rows], axis=0)


def body(coefficients, positions, polar, azimuth, weights, farmap, dir_sizes, dom_size):
    own_count = coefficients.shape[2]
    dir_size = dir_sizes[0] * dir_sizes[1]
    own_rows = coefficients.reshape(2 * C, own_count)
    place_blocks = gather_blocks(positions, DIR_AXES, dir_size)
    domain_places = jnp.moveaxis(place_blocks, 0, 1).reshape(3, dir_size * own_count)
    own_rows, domain_places = lax.optimization_barrier((own_rows, domain_places))
    coef_blocks = gather_blocks(own_rows, DIR_AXES, dir_size)
    domain_rows = jnp.moveaxis(coef_blocks, 0, 1).reshape(2 * C, dir_size * own_count)
    vectors = unit_vectors(polar, azimuth)
    cos_tile, sin_tile = phase_tile(domain_places, vectors)
    partial_fields = field_terms(domain_rows, cos_tile, sin_tile)
    dir_count = polar.shape[0]
    slice_width = dir_count // dom_size
    fields_slice = scatter_sum(partial_fields, DOM_AXES, dom_size)
    offset = lax.axis_index(DOM_AXES) * slice_width
    farmap_slice = lax.dynamic_slice_in_dim(farmap, offset, slice_width, 3)
    weights_slice = lax.dynamic_slice_in_dim(weights, offset, slice_width, 0)
    adjoint_slice = cotangent_rows(fields_slice, farmap_slice, weights_slice)
    adjoint_blocks = gather_blocks(adjoint_slice, DOM_AXES, dom_size)
    adjoint = jnp.moveaxis(adjoint_blocks, 0, 1).reshape(2 * C, dir_count)
    stacked = stacked_rows(adjoint, vectors)
    coef_part, place_part = gradients(adjoint_terms(stacked, cos_tile, sin_tile), domain_rows)
    part = jnp.concatenate([coef_part, place_part], axis=0)
    reduced = scatter_dir(part, dir_sizes)
    return (reduced[: 2 * C].reshape(2, C, own_count), reduced[2 * C :])


def solution(mesh):
    dom_size = mesh.shape["dom"]
    dir_size = mesh.shape["dir"]
    chips_z = 2 if dom_size % 4 == 0 else 1
    dom_sizes = (dom_size // (2 * chips_z), chips_z, 2)
    x_size = 4 if dir_size % 4 == 0 else dir_size
    dir_sizes = (x_size, dir_size // x_size)
    fine = jax.sharding.Mesh(
        mesh.devices.reshape(dom_sizes + dir_sizes), DOM_AXES + DIR_AXES
    )
    every = DOM_AXES + DIR_AXES
    placed = (
        P(None, None, every),
        P(None, every),
        P(DIR_AXES),
        P(DIR_AXES),
        P(DIR_AXES),
        P(None, None, None, DIR_AXES),
    )
    return jax.shard_map(
        functools.partial(body, dir_sizes=dir_sizes, dom_size=dom_size),
        mesh=fine,
        in_specs=placed,
        out_specs=(P(None, None, every), P(None, every)),
        check_vma=False,
    )
```

```python
import functools

import jax
import jax.numpy as jnp
from jax import lax
import numpy as np
from jax.sharding import PartitionSpec as P

C = 70


def unit_vectors(polar, azimuth):
    sine_polar = jnp.sin(polar)
    return jnp.stack([sine_polar * jnp.cos(azimuth), sine_polar * jnp.sin(azimuth), jnp.cos(polar)])


def sine_cosine(angles):
    quarter = jnp.round(angles * np.float32(2.0 / np.pi))
    reduced = angles - quarter * np.float32(1.5703125)
    reduced = reduced - quarter * np.float32(4.837512969970703125e-4)
    reduced = reduced - quarter * np.float32(7.54978995489188216e-8)
    square = reduced * reduced
    sine = reduced + reduced * square * (
        np.float32(-1 / 6)
        + square * (np.float32(1 / 120) + square * (np.float32(-1 / 5040) + square * np.float32(1 / 362880)))
    )
    cosine = np.float32(1) + square * (
        np.float32(-0.5)
        + square * (np.float32(1 / 24) + square * (np.float32(-1 / 720) + square * np.float32(1 / 40320)))
    )
    turn = quarter.astype(jnp.int32)
    odd = (turn & 1) == 1
    cos_base = jnp.where(odd, sine, cosine)
    sin_base = jnp.where(odd, cosine, sine)
    cos_value = jnp.where(((turn + 1) & 2) == 2, -cos_base, cos_base)
    sin_value = jnp.where((turn & 2) == 2, -sin_base, sin_base)
    return (cos_value, sin_value)


def phase_tile(places, vectors):
    angles = (
        places[0][:, None] * vectors[0][None, :]
        + places[1][:, None] * vectors[1][None, :]
        + places[2][:, None] * vectors[2][None, :]
    )
    cos_value, sin_value = sine_cosine(angles)
    return (cos_value.astype(jnp.bfloat16), sin_value.astype(jnp.bfloat16))


def field_terms(coef_block, cos_tile, sin_tile):
    order_count = coef_block.shape[0] // 2
    real_rows = coef_block[:order_count]
    imag_rows = coef_block[order_count:]
    top_rows = jnp.concatenate([real_rows, imag_rows], axis=1)
    low_rows = jnp.concatenate([imag_rows, -real_rows], axis=1)
    left_side = jnp.concatenate([top_rows, low_rows], axis=0)
    right_side = jnp.concatenate([cos_tile, sin_tile], axis=0)
    return jnp.dot(left_side, right_side, preferred_element_type=jnp.float32)


def adjoint_terms(stacked, cos_tile, sin_tile):
    order_count = stacked.shape[0] // 2
    real_rows = stacked[:order_count]
    imag_rows = stacked[order_count:]
    top_rows = jnp.concatenate([real_rows, imag_rows], axis=1)
    low_rows = jnp.concatenate([imag_rows, -real_rows], axis=1)
    left_side = jnp.concatenate([top_rows, low_rows], axis=0)
    right_side = jnp.concatenate([cos_tile, sin_tile], axis=1)
    return lax.dot_general(
        left_side, right_side, (((1,), (1,)), ((), ())), preferred_element_type=jnp.float32
    )


def amplitude_parts(fields, farmap):
    order_count = fields.shape[0] // 2
    field_real = fields[:order_count][None]
    field_imag = fields[order_count:][None]
    map_real = farmap[:, 0]
    map_imag = farmap[:, 1]
    amp_real = jnp.sum(map_real * field_real - map_imag * field_imag, axis=1)
    amp_imag = jnp.sum(map_real * field_imag + map_imag * field_real, axis=1)
    return (amp_real, amp_imag)


def cotangent_from(amp_real, amp_imag, farmap, weights):
    map_real = farmap[:, 0]
    map_imag = farmap[:, 1]
    cot_real = weights * jnp.sum(
        amp_real[:, None] * map_real + amp_imag[:, None] * map_imag, axis=0
    )
    cot_imag = weights * jnp.sum(
        amp_real[:, None] * map_imag - amp_imag[:, None] * map_real, axis=0
    )
    return jnp.concatenate([cot_real, cot_imag], axis=0).astype(jnp.bfloat16)


def cotangent_rows(fields, farmap, weights):
    amp_real, amp_imag = amplitude_parts(fields, farmap)
    return cotangent_from(amp_real, amp_imag, farmap, weights)


def stacked_rows(adjoint, vectors):
    order_count = adjoint.shape[0] // 2
    widened = adjoint.astype(jnp.float32)
    scaled = [(vectors[axis_id][None, :] * widened).astype(jnp.bfloat16) for axis_id in range(3)]
    real_parts = [adjoint[:order_count]] + [item[:order_count] for item in scaled]
    imag_parts = [adjoint[order_count:]] + [item[order_count:] for item in scaled]
    return jnp.concatenate(real_parts + imag_parts, axis=0)


def gradients(output, coef_block):
    order_count = coef_block.shape[0] // 2
    real_out = output[: 4 * order_count]
    imag_out = output[4 * order_count :]
    coef_term = jnp.concatenate(
        [2.0 * real_out[:order_count], -2.0 * imag_out[:order_count]], axis=0
    )
    coef_real = coef_block[:order_count].astype(jnp.float32)
    coef_imag = coef_block[order_count:].astype(jnp.float32)
    place_terms = []
    for axis_id in range(3):
        lower_row = (axis_id + 1) * order_count
        upper_row = (axis_id + 2) * order_count
        place_terms.append(
            2.0
            * jnp.sum(
                coef_real * imag_out[lower_row:upper_row]
                + coef_imag * real_out[lower_row:upper_row],
                axis=0,
            )
        )
    return (coef_term, jnp.stack(place_terms))


DOM_AXES = ("y", "z_lo", "core")
DIR_AXES = ("x", "z_hi")


def gather_blocks(block, axis_name, size):
    spread = jnp.broadcast_to(block[None], (size,) + block.shape)
    return lax.all_to_all(spread, axis_name, 0, 0, tiled=True)


def scatter_sum(part, axis_name, size):
    rows, width = part.shape
    split = part.reshape(rows, size, width // size)
    received = lax.all_to_all(split, axis_name, 1, 1, tiled=True)
    return jnp.sum(received, axis=1)


def scatter_dir(part, sizes):
    rows, width = part.shape
    size = sizes[0] * sizes[1]
    split = part.reshape(rows, size, width // size)
    received = lax.all_to_all(narrow_rows(split), DIR_AXES, 1, 1, tiled=True)
    return jnp.sum(widen_rows(received), axis=1)


def narrow_rows(part):
    coef_rows = part[: 2 * C].astype(jnp.bfloat16)
    place_high = part[2 * C :].astype(jnp.bfloat16)
    place_low = (part[2 * C :] - place_high.astype(jnp.float32)).astype(jnp.bfloat16)
    return jnp.concatenate([coef_rows, place_high, place_low], axis=0)


def widen_rows(packed):
    wide = packed.astype(jnp.float32)
    place_count = (packed.shape[0] - 2 * C) // 2
    place_rows = wide[2 * C : 2 * C + place_count] + wide[2 * C + place_count :]
    return jnp.concatenate([wide[: 2 * C], place_rows], axis=0)


def body(coefficients, positions, polar, azimuth, weights, farmap, dir_sizes, dom_size):
    own_count = coefficients.shape[2]
    dir_size = dir_sizes[0] * dir_sizes[1]
    own_rows = coefficients.reshape(2 * C, own_count)
    coef_blocks = gather_blocks(own_rows, DIR_AXES, dir_size)
    domain_rows = jnp.moveaxis(coef_blocks, 0, 1).reshape(2 * C, dir_size * own_count)
    positions, domain_rows = lax.optimization_barrier((positions, domain_rows))
    place_blocks = gather_blocks(positions, DIR_AXES, dir_size)
    domain_places = jnp.moveaxis(place_blocks, 0, 1).reshape(3, dir_size * own_count)
    vectors = unit_vectors(polar, azimuth)
    cos_tile, sin_tile = phase_tile(domain_places, vectors)
    partial_fields = field_terms(domain_rows, cos_tile, sin_tile)
    dir_count = polar.shape[0]
    slice_width = dir_count // dom_size
    fields_slice = scatter_sum(partial_fields, DOM_AXES, dom_size)
    offset = lax.axis_index(DOM_AXES) * slice_width
    farmap_slice = lax.dynamic_slice_in_dim(farmap, offset, slice_width, 3)
    weights_slice = lax.dynamic_slice_in_dim(weights, offset, slice_width, 0)
    adjoint_slice = cotangent_rows(fields_slice, farmap_slice, weights_slice)
    adjoint_blocks = gather_blocks(adjoint_slice, DOM_AXES, dom_size)
    adjoint = jnp.moveaxis(adjoint_blocks, 0, 1).reshape(2 * C, dir_count)
    stacked = stacked_rows(adjoint, vectors)
    coef_part, place_part = gradients(adjoint_terms(stacked, cos_tile, sin_tile), domain_rows)
    part = jnp.concatenate([coef_part, place_part], axis=0)
    reduced = scatter_dir(part, dir_sizes)
    return (reduced[: 2 * C].reshape(2, C, own_count), reduced[2 * C :])


def solution(mesh):
    dom_size = mesh.shape["dom"]
    dir_size = mesh.shape["dir"]
    chips_z = 2 if dom_size % 4 == 0 else 1
    dom_sizes = (dom_size // (2 * chips_z), chips_z, 2)
    x_size = 4 if dir_size % 4 == 0 else dir_size
    dir_sizes = (x_size, dir_size // x_size)
    fine = jax.sharding.Mesh(
        mesh.devices.reshape(dom_sizes + dir_sizes), DOM_AXES + DIR_AXES
    )
    every = DOM_AXES + DIR_AXES
    placed = (
        P(None, None, every),
        P(None, every),
        P(DIR_AXES),
        P(DIR_AXES),
        P(DIR_AXES),
        P(None, None, None, DIR_AXES),
    )
    return jax.shard_map(
        functools.partial(body, dir_sizes=dir_sizes, dom_size=dom_size),
        mesh=fine,
        in_specs=placed,
        out_specs=(P(None, None, every), P(None, every)),
        check_vma=False,
    )
```

```python
import functools

import jax
import jax.numpy as jnp
from jax import lax
import numpy as np
from jax.sharding import PartitionSpec as P

C = 70


def unit_vectors(polar, azimuth):
    sine_polar = jnp.sin(polar)
    return jnp.stack([sine_polar * jnp.cos(azimuth), sine_polar * jnp.sin(azimuth), jnp.cos(polar)])


def sine_cosine(angles):
    quarter = jnp.round(angles * np.float32(2.0 / np.pi))
    reduced = angles - quarter * np.float32(1.5703125)
    reduced = reduced - quarter * np.float32(4.837512969970703125e-4)
    reduced = reduced - quarter * np.float32(7.54978995489188216e-8)
    square = reduced * reduced
    sine = reduced + reduced * square * (
        np.float32(-1 / 6)
        + square * (np.float32(1 / 120) + square * (np.float32(-1 / 5040) + square * np.float32(1 / 362880)))
    )
    cosine = np.float32(1) + square * (
        np.float32(-0.5)
        + square * (np.float32(1 / 24) + square * (np.float32(-1 / 720) + square * np.float32(1 / 40320)))
    )
    turn = quarter.astype(jnp.int32)
    odd = (turn & 1) == 1
    cos_base = jnp.where(odd, sine, cosine)
    sin_base = jnp.where(odd, cosine, sine)
    cos_value = jnp.where(((turn + 1) & 2) == 2, -cos_base, cos_base)
    sin_value = jnp.where((turn & 2) == 2, -sin_base, sin_base)
    return (cos_value, sin_value)


def phase_tile(places, vectors):
    angles = (
        places[0][:, None] * vectors[0][None, :]
        + places[1][:, None] * vectors[1][None, :]
        + places[2][:, None] * vectors[2][None, :]
    )
    cos_value, sin_value = sine_cosine(angles)
    return (cos_value.astype(jnp.bfloat16), sin_value.astype(jnp.bfloat16))


def field_terms(coef_block, cos_tile, sin_tile):
    order_count = coef_block.shape[0] // 2
    real_rows = coef_block[:order_count]
    imag_rows = coef_block[order_count:]
    top_rows = jnp.concatenate([real_rows, imag_rows], axis=1)
    low_rows = jnp.concatenate([imag_rows, -real_rows], axis=1)
    left_side = jnp.concatenate([top_rows, low_rows], axis=0)
    right_side = jnp.concatenate([cos_tile, sin_tile], axis=0)
    return jnp.dot(left_side, right_side, preferred_element_type=jnp.float32)


def adjoint_terms(stacked, cos_tile, sin_tile):
    order_count = stacked.shape[0] // 2
    real_rows = stacked[:order_count]
    imag_rows = stacked[order_count:]
    top_rows = jnp.concatenate([real_rows, imag_rows], axis=1)
    low_rows = jnp.concatenate([imag_rows, -real_rows], axis=1)
    left_side = jnp.concatenate([top_rows, low_rows], axis=0)
    right_side = jnp.concatenate([cos_tile, sin_tile], axis=1)
    return lax.dot_general(
        left_side, right_side, (((1,), (1,)), ((), ())), preferred_element_type=jnp.float32
    )


def amplitude_parts(fields, farmap):
    order_count = fields.shape[0] // 2
    field_real = fields[:order_count][None]
    field_imag = fields[order_count:][None]
    map_real = farmap[:, 0]
    map_imag = farmap[:, 1]
    amp_real = jnp.sum(map_real * field_real - map_imag * field_imag, axis=1)
    amp_imag = jnp.sum(map_real * field_imag + map_imag * field_real, axis=1)
    return (amp_real, amp_imag)


def cotangent_from(amp_real, amp_imag, farmap, weights):
    map_real = farmap[:, 0]
    map_imag = farmap[:, 1]
    cot_real = weights * jnp.sum(
        amp_real[:, None] * map_real + amp_imag[:, None] * map_imag, axis=0
    )
    cot_imag = weights * jnp.sum(
        amp_real[:, None] * map_imag - amp_imag[:, None] * map_real, axis=0
    )
    return jnp.concatenate([cot_real, cot_imag], axis=0).astype(jnp.bfloat16)


def cotangent_rows(fields, farmap, weights):
    amp_real, amp_imag = amplitude_parts(fields, farmap)
    return cotangent_from(amp_real, amp_imag, farmap, weights)


def stacked_rows(adjoint, vectors):
    order_count = adjoint.shape[0] // 2
    widened = adjoint.astype(jnp.float32)
    scaled = [(vectors[axis_id][None, :] * widened).astype(jnp.bfloat16) for axis_id in range(3)]
    real_parts = [adjoint[:order_count]] + [item[:order_count] for item in scaled]
    imag_parts = [adjoint[order_count:]] + [item[order_count:] for item in scaled]
    return jnp.concatenate(real_parts + imag_parts, axis=0)


def gradients(output, coef_block):
    order_count = coef_block.shape[0] // 2
    real_out = output[: 4 * order_count]
    imag_out = output[4 * order_count :]
    coef_term = jnp.concatenate(
        [2.0 * real_out[:order_count], -2.0 * imag_out[:order_count]], axis=0
    )
    coef_real = coef_block[:order_count].astype(jnp.float32)
    coef_imag = coef_block[order_count:].astype(jnp.float32)
    place_terms = []
    for axis_id in range(3):
        lower_row = (axis_id + 1) * order_count
        upper_row = (axis_id + 2) * order_count
        place_terms.append(
            2.0
            * jnp.sum(
                coef_real * imag_out[lower_row:upper_row]
                + coef_imag * real_out[lower_row:upper_row],
                axis=0,
            )
        )
    return (coef_term, jnp.stack(place_terms))


DOM_AXES = ("y", "z_lo", "core")
DIR_AXES = ("x", "z_hi")


def gather_blocks(block, axis_name, size):
    spread = jnp.broadcast_to(block[None], (size,) + block.shape)
    return lax.all_to_all(spread, axis_name, 0, 0, tiled=True)


def scatter_sum(part, axis_name, size):
    rows, width = part.shape
    split = part.reshape(rows, size, width // size)
    received = lax.all_to_all(split, axis_name, 1, 1, tiled=True)
    return jnp.sum(received, axis=1)


def scatter_dir(part, sizes):
    rows, width = part.shape
    size = sizes[0] * sizes[1]
    split = part.reshape(rows, size, width // size)
    received = lax.all_to_all(narrow_rows(split), DIR_AXES, 1, 1, tiled=True)
    return jnp.sum(widen_rows(received), axis=1)


def narrow_rows(part):
    coef_rows = part[: 2 * C].astype(jnp.bfloat16)
    place_high = part[2 * C :].astype(jnp.bfloat16)
    place_low = (part[2 * C :] - place_high.astype(jnp.float32)).astype(jnp.bfloat16)
    return jnp.concatenate([coef_rows, place_high, place_low], axis=0)


def widen_rows(packed):
    wide = packed.astype(jnp.float32)
    place_count = (packed.shape[0] - 2 * C) // 2
    place_rows = wide[2 * C : 2 * C + place_count] + wide[2 * C + place_count :]
    return jnp.concatenate([wide[: 2 * C], place_rows], axis=0)


def body(coefficients, positions, polar, azimuth, weights, farmap, dir_sizes, dom_size):
    own_count = coefficients.shape[2]
    dir_size = dir_sizes[0] * dir_sizes[1]
    own_rows = coefficients.reshape(2 * C, own_count)
    place_blocks = gather_blocks(positions, DIR_AXES, dir_size)
    domain_places = jnp.moveaxis(place_blocks, 0, 1).reshape(3, dir_size * own_count)
    own_rows, domain_places = lax.optimization_barrier((own_rows, domain_places))
    coef_blocks = gather_blocks(own_rows, DIR_AXES, dir_size)
    domain_rows = jnp.moveaxis(coef_blocks, 0, 1).reshape(2 * C, dir_size * own_count)
    vectors = unit_vectors(polar, azimuth)
    cos_tile, sin_tile = phase_tile(domain_places, vectors)
    partial_fields = field_terms(domain_rows, cos_tile, sin_tile)
    dir_count = polar.shape[0]
    slice_width = dir_count // dom_size
    flat_fields = jnp.transpose(
        partial_fields.reshape(2 * C, dom_size, slice_width), (1, 0, 2)
    ).reshape(dom_size, 2 * C * slice_width)
    received_fields = lax.all_to_all(flat_fields, DOM_AXES, 0, 0, tiled=True)
    fields_slice = jnp.sum(received_fields, axis=0).reshape(2 * C, slice_width)
    offset = lax.axis_index(DOM_AXES) * slice_width
    farmap_slice = lax.dynamic_slice_in_dim(farmap, offset, slice_width, 3)
    weights_slice = lax.dynamic_slice_in_dim(weights, offset, slice_width, 0)
    adjoint_slice = cotangent_rows(fields_slice, farmap_slice, weights_slice)
    adjoint_blocks = gather_blocks(adjoint_slice.reshape(2 * C * slice_width), DOM_AXES, dom_size)
    adjoint = jnp.transpose(
        adjoint_blocks.reshape(dom_size, 2 * C, slice_width), (1, 0, 2)
    ).reshape(2 * C, dir_count)
    stacked = stacked_rows(adjoint, vectors)
    coef_part, place_part = gradients(adjoint_terms(stacked, cos_tile, sin_tile), domain_rows)
    part = jnp.concatenate([coef_part, place_part], axis=0)
    reduced = scatter_dir(part, dir_sizes)
    return (reduced[: 2 * C].reshape(2, C, own_count), reduced[2 * C :])


def solution(mesh):
    dom_size = mesh.shape["dom"]
    dir_size = mesh.shape["dir"]
    chips_z = 2 if dom_size % 4 == 0 else 1
    dom_sizes = (dom_size // (2 * chips_z), chips_z, 2)
    x_size = 4 if dir_size % 4 == 0 else dir_size
    dir_sizes = (x_size, dir_size // x_size)
    fine = jax.sharding.Mesh(
        mesh.devices.reshape(dom_sizes + dir_sizes), DOM_AXES + DIR_AXES
    )
    every = DOM_AXES + DIR_AXES
    placed = (
        P(None, None, every),
        P(None, every),
        P(DIR_AXES),
        P(DIR_AXES),
        P(DIR_AXES),
        P(None, None, None, DIR_AXES),
    )
    return jax.shard_map(
        functools.partial(body, dir_sizes=dir_sizes, dom_size=dom_size),
        mesh=fine,
        in_specs=placed,
        out_specs=(P(None, None, every), P(None, every)),
        check_vma=False,
    )
```

```python
import functools

import jax
import jax.numpy as jnp
from jax import lax
import numpy as np
from jax.sharding import PartitionSpec as P

C = 70


def unit_vectors(polar, azimuth):
    sine_polar = jnp.sin(polar)
    return jnp.stack([sine_polar * jnp.cos(azimuth), sine_polar * jnp.sin(azimuth), jnp.cos(polar)])


def sine_cosine(angles):
    quarter = jnp.round(angles * np.float32(2.0 / np.pi))
    reduced = angles - quarter * np.float32(1.5703125)
    reduced = reduced - quarter * np.float32(4.837512969970703125e-4)
    reduced = reduced - quarter * np.float32(7.54978995489188216e-8)
    square = reduced * reduced
    sine = reduced + reduced * square * (
        np.float32(-1 / 6)
        + square * (np.float32(1 / 120) + square * (np.float32(-1 / 5040) + square * np.float32(1 / 362880)))
    )
    cosine = np.float32(1) + square * (
        np.float32(-0.5)
        + square * (np.float32(1 / 24) + square * (np.float32(-1 / 720) + square * np.float32(1 / 40320)))
    )
    turn = quarter.astype(jnp.int32)
    odd = (turn & 1) == 1
    cos_base = jnp.where(odd, sine, cosine)
    sin_base = jnp.where(odd, cosine, sine)
    cos_value = jnp.where(((turn + 1) & 2) == 2, -cos_base, cos_base)
    sin_value = jnp.where((turn & 2) == 2, -sin_base, sin_base)
    return (cos_value, sin_value)


def phase_tile(places, vectors):
    angles = (
        places[0][:, None] * vectors[0][None, :]
        + places[1][:, None] * vectors[1][None, :]
        + places[2][:, None] * vectors[2][None, :]
    )
    cos_value, sin_value = sine_cosine(angles)
    return (cos_value.astype(jnp.bfloat16), sin_value.astype(jnp.bfloat16))


def field_terms(coef_block, cos_tile, sin_tile):
    order_count = coef_block.shape[0] // 2
    real_rows = coef_block[:order_count]
    imag_rows = coef_block[order_count:]
    top_rows = jnp.concatenate([real_rows, imag_rows], axis=1)
    low_rows = jnp.concatenate([imag_rows, -real_rows], axis=1)
    left_side = jnp.concatenate([top_rows, low_rows], axis=0)
    right_side = jnp.concatenate([cos_tile, sin_tile], axis=0)
    return jnp.dot(left_side, right_side, preferred_element_type=jnp.float32)


def adjoint_terms(stacked, cos_tile, sin_tile):
    order_count = stacked.shape[0] // 2
    real_rows = stacked[:order_count]
    imag_rows = stacked[order_count:]
    top_rows = jnp.concatenate([real_rows, imag_rows], axis=1)
    low_rows = jnp.concatenate([imag_rows, -real_rows], axis=1)
    left_side = jnp.concatenate([top_rows, low_rows], axis=0)
    right_side = jnp.concatenate([cos_tile, sin_tile], axis=1)
    return lax.dot_general(
        left_side, right_side, (((1,), (1,)), ((), ())), preferred_element_type=jnp.float32
    )


def amplitude_parts(fields, farmap):
    order_count = fields.shape[0] // 2
    field_real = fields[:order_count][None]
    field_imag = fields[order_count:][None]
    map_real = farmap[:, 0]
    map_imag = farmap[:, 1]
    amp_real = jnp.sum(map_real * field_real - map_imag * field_imag, axis=1)
    amp_imag = jnp.sum(map_real * field_imag + map_imag * field_real, axis=1)
    return (amp_real, amp_imag)


def cotangent_from(amp_real, amp_imag, farmap, weights):
    map_real = farmap[:, 0]
    map_imag = farmap[:, 1]
    cot_real = weights * jnp.sum(
        amp_real[:, None] * map_real + amp_imag[:, None] * map_imag, axis=0
    )
    cot_imag = weights * jnp.sum(
        amp_real[:, None] * map_imag - amp_imag[:, None] * map_real, axis=0
    )
    return jnp.concatenate([cot_real, cot_imag], axis=0).astype(jnp.bfloat16)


def cotangent_rows(fields, farmap, weights):
    amp_real, amp_imag = amplitude_parts(fields, farmap)
    return cotangent_from(amp_real, amp_imag, farmap, weights)


def stacked_rows(adjoint, vectors):
    order_count = adjoint.shape[0] // 2
    widened = adjoint.astype(jnp.float32)
    scaled = [(vectors[axis_id][None, :] * widened).astype(jnp.bfloat16) for axis_id in range(3)]
    real_parts = [adjoint[:order_count]] + [item[:order_count] for item in scaled]
    imag_parts = [adjoint[order_count:]] + [item[order_count:] for item in scaled]
    return jnp.concatenate(real_parts + imag_parts, axis=0)


def gradients(output, coef_block):
    order_count = coef_block.shape[0] // 2
    real_out = output[: 4 * order_count]
    imag_out = output[4 * order_count :]
    coef_term = jnp.concatenate(
        [2.0 * real_out[:order_count], -2.0 * imag_out[:order_count]], axis=0
    )
    coef_real = coef_block[:order_count].astype(jnp.float32)
    coef_imag = coef_block[order_count:].astype(jnp.float32)
    place_terms = []
    for axis_id in range(3):
        lower_row = (axis_id + 1) * order_count
        upper_row = (axis_id + 2) * order_count
        place_terms.append(
            2.0
            * jnp.sum(
                coef_real * imag_out[lower_row:upper_row]
                + coef_imag * real_out[lower_row:upper_row],
                axis=0,
            )
        )
    return (coef_term, jnp.stack(place_terms))


DOM_AXES = ("y", "z_lo", "core")
DIR_AXES = ("x", "z_hi")


def gather_blocks(block, axis_name, size):
    spread = jnp.broadcast_to(block[None], (size,) + block.shape)
    return lax.all_to_all(spread, axis_name, 0, 0, tiled=True)


def scatter_sum(part, axis_name, size, sum_type=None):
    rows, width = part.shape
    split = part.reshape(rows, size, width // size)
    received = lax.all_to_all(split, axis_name, 1, 1, tiled=True)
    return jnp.sum(received.astype(sum_type or received.dtype), axis=1)


def scatter_dir(part, sizes):
    rows, width = part.shape
    size = sizes[0] * sizes[1]
    split = part.reshape(rows, size, width // size)
    received = lax.all_to_all(narrow_rows(split), DIR_AXES, 1, 1, tiled=True)
    return jnp.sum(widen_rows(received), axis=1)


def narrow_rows(part):
    coef_rows = part[: 2 * C].astype(jnp.bfloat16)
    place_high = part[2 * C :].astype(jnp.bfloat16)
    place_low = (part[2 * C :] - place_high.astype(jnp.float32)).astype(jnp.bfloat16)
    return jnp.concatenate([coef_rows, place_high, place_low], axis=0)


def widen_rows(packed):
    wide = packed.astype(jnp.float32)
    place_count = (packed.shape[0] - 2 * C) // 2
    place_rows = wide[2 * C : 2 * C + place_count] + wide[2 * C + place_count :]
    return jnp.concatenate([wide[: 2 * C], place_rows], axis=0)


def body(coefficients, positions, polar, azimuth, weights, farmap, dir_sizes, dom_size):
    own_count = coefficients.shape[2]
    dir_size = dir_sizes[0] * dir_sizes[1]
    own_rows = coefficients.reshape(2 * C, own_count)
    place_blocks = gather_blocks(positions, DIR_AXES, dir_size)
    domain_places = jnp.moveaxis(place_blocks, 0, 1).reshape(3, dir_size * own_count)
    own_rows, domain_places = lax.optimization_barrier((own_rows, domain_places))
    coef_blocks = gather_blocks(own_rows, DIR_AXES, dir_size)
    domain_rows = jnp.moveaxis(coef_blocks, 0, 1).reshape(2 * C, dir_size * own_count)
    vectors = unit_vectors(polar, azimuth)
    cos_tile, sin_tile = phase_tile(domain_places, vectors)
    partial_fields = field_terms(domain_rows, cos_tile, sin_tile)
    dir_count = polar.shape[0]
    slice_width = dir_count // dom_size
    fields_slice = scatter_sum(partial_fields.astype(jnp.bfloat16), DOM_AXES, dom_size, jnp.float32)
    offset = lax.axis_index(DOM_AXES) * slice_width
    farmap_slice = lax.dynamic_slice_in_dim(farmap, offset, slice_width, 3)
    weights_slice = lax.dynamic_slice_in_dim(weights, offset, slice_width, 0)
    adjoint_slice = cotangent_rows(fields_slice, farmap_slice, weights_slice)
    adjoint_blocks = gather_blocks(adjoint_slice, DOM_AXES, dom_size)
    adjoint = jnp.moveaxis(adjoint_blocks, 0, 1).reshape(2 * C, dir_count)
    stacked = stacked_rows(adjoint, vectors)
    coef_part, place_part = gradients(adjoint_terms(stacked, cos_tile, sin_tile), domain_rows)
    part = jnp.concatenate([coef_part, place_part], axis=0)
    reduced = scatter_dir(part, dir_sizes)
    return (reduced[: 2 * C].reshape(2, C, own_count), reduced[2 * C :])


def solution(mesh):
    dom_size = mesh.shape["dom"]
    dir_size = mesh.shape["dir"]
    chips_z = 2 if dom_size % 4 == 0 else 1
    dom_sizes = (dom_size // (2 * chips_z), chips_z, 2)
    x_size = 4 if dir_size % 4 == 0 else dir_size
    dir_sizes = (x_size, dir_size // x_size)
    fine = jax.sharding.Mesh(
        mesh.devices.reshape(dom_sizes + dir_sizes), DOM_AXES + DIR_AXES
    )
    every = DOM_AXES + DIR_AXES
    placed = (
        P(None, None, every),
        P(None, every),
        P(DIR_AXES),
        P(DIR_AXES),
        P(DIR_AXES),
        P(None, None, None, DIR_AXES),
    )
    return jax.shard_map(
        functools.partial(body, dir_sizes=dir_sizes, dom_size=dom_size),
        mesh=fine,
        in_specs=placed,
        out_specs=(P(None, None, every), P(None, every)),
        check_vma=False,
    )
```

```python
import functools

import jax
import jax.numpy as jnp
from jax import lax
import numpy as np
from jax.sharding import PartitionSpec as P

C = 70


def unit_vectors(polar, azimuth):
    sine_polar = jnp.sin(polar)
    return jnp.stack([sine_polar * jnp.cos(azimuth), sine_polar * jnp.sin(azimuth), jnp.cos(polar)])


def sine_cosine(angles):
    quarter = jnp.round(angles * np.float32(2.0 / np.pi))
    reduced = angles - quarter * np.float32(1.5703125)
    reduced = reduced - quarter * np.float32(4.837512969970703125e-4)
    reduced = reduced - quarter * np.float32(7.54978995489188216e-8)
    square = reduced * reduced
    sine = reduced + reduced * square * (
        np.float32(-1 / 6)
        + square * (np.float32(1 / 120) + square * (np.float32(-1 / 5040) + square * np.float32(1 / 362880)))
    )
    cosine = np.float32(1) + square * (
        np.float32(-0.5)
        + square * (np.float32(1 / 24) + square * (np.float32(-1 / 720) + square * np.float32(1 / 40320)))
    )
    turn = quarter.astype(jnp.int32)
    odd = (turn & 1) == 1
    cos_base = jnp.where(odd, sine, cosine)
    sin_base = jnp.where(odd, cosine, sine)
    cos_value = jnp.where(((turn + 1) & 2) == 2, -cos_base, cos_base)
    sin_value = jnp.where((turn & 2) == 2, -sin_base, sin_base)
    return (cos_value, sin_value)


def phase_tile(places, vectors):
    angles = (
        places[0][:, None] * vectors[0][None, :]
        + places[1][:, None] * vectors[1][None, :]
        + places[2][:, None] * vectors[2][None, :]
    )
    cos_value, sin_value = sine_cosine(angles)
    return (cos_value.astype(jnp.bfloat16), sin_value.astype(jnp.bfloat16))


def field_terms(coef_block, cos_tile, sin_tile):
    order_count = coef_block.shape[0] // 2
    real_rows = coef_block[:order_count]
    imag_rows = coef_block[order_count:]
    top_rows = jnp.concatenate([real_rows, imag_rows], axis=1)
    low_rows = jnp.concatenate([imag_rows, -real_rows], axis=1)
    left_side = jnp.concatenate([top_rows, low_rows], axis=0)
    right_side = jnp.concatenate([cos_tile, sin_tile], axis=0)
    return jnp.dot(left_side, right_side, preferred_element_type=jnp.float32)


def adjoint_terms(stacked, cos_tile, sin_tile):
    order_count = stacked.shape[0] // 2
    real_rows = stacked[:order_count]
    imag_rows = stacked[order_count:]
    top_rows = jnp.concatenate([real_rows, imag_rows], axis=1)
    low_rows = jnp.concatenate([imag_rows, -real_rows], axis=1)
    left_side = jnp.concatenate([top_rows, low_rows], axis=0)
    right_side = jnp.concatenate([cos_tile, sin_tile], axis=1)
    return lax.dot_general(
        left_side, right_side, (((1,), (1,)), ((), ())), preferred_element_type=jnp.float32
    )


def amplitude_parts(fields, farmap):
    order_count = fields.shape[0] // 2
    field_real = fields[:order_count][None]
    field_imag = fields[order_count:][None]
    map_real = farmap[:, 0]
    map_imag = farmap[:, 1]
    amp_real = jnp.sum(map_real * field_real - map_imag * field_imag, axis=1)
    amp_imag = jnp.sum(map_real * field_imag + map_imag * field_real, axis=1)
    return (amp_real, amp_imag)


def cotangent_from(amp_real, amp_imag, farmap, weights):
    map_real = farmap[:, 0]
    map_imag = farmap[:, 1]
    cot_real = weights * jnp.sum(
        amp_real[:, None] * map_real + amp_imag[:, None] * map_imag, axis=0
    )
    cot_imag = weights * jnp.sum(
        amp_real[:, None] * map_imag - amp_imag[:, None] * map_real, axis=0
    )
    return jnp.concatenate([cot_real, cot_imag], axis=0).astype(jnp.bfloat16)


def cotangent_rows(fields, farmap, weights):
    amp_real, amp_imag = amplitude_parts(fields, farmap)
    return cotangent_from(amp_real, amp_imag, farmap, weights)


def stacked_rows(adjoint, vectors):
    order_count = adjoint.shape[0] // 2
    widened = adjoint.astype(jnp.float32)
    scaled = [(vectors[axis_id][None, :] * widened).astype(jnp.bfloat16) for axis_id in range(3)]
    real_parts = [adjoint[:order_count]] + [item[:order_count] for item in scaled]
    imag_parts = [adjoint[order_count:]] + [item[order_count:] for item in scaled]
    return jnp.concatenate(real_parts + imag_parts, axis=0)


def gradients(output, coef_block):
    order_count = coef_block.shape[0] // 2
    real_out = output[: 4 * order_count]
    imag_out = output[4 * order_count :]
    coef_term = jnp.concatenate(
        [2.0 * real_out[:order_count], -2.0 * imag_out[:order_count]], axis=0
    )
    coef_real = coef_block[:order_count].astype(jnp.float32)
    coef_imag = coef_block[order_count:].astype(jnp.float32)
    place_terms = []
    for axis_id in range(3):
        lower_row = (axis_id + 1) * order_count
        upper_row = (axis_id + 2) * order_count
        place_terms.append(
            2.0
            * jnp.sum(
                coef_real * imag_out[lower_row:upper_row]
                + coef_imag * real_out[lower_row:upper_row],
                axis=0,
            )
        )
    return (coef_term, jnp.stack(place_terms))


DOM_AXES = ("y", "z_lo", "core")
DIR_AXES = ("x", "z_hi")


def gather_blocks(block, axis_name, size):
    spread = jnp.broadcast_to(block[None], (size,) + block.shape)
    return lax.all_to_all(spread, axis_name, 0, 0, tiled=True)


def scatter_sum(part, axis_name, size, sum_type=None):
    rows, width = part.shape
    split = part.reshape(rows, size, width // size)
    received = lax.all_to_all(split, axis_name, 1, 1, tiled=True)
    return jnp.sum(received.astype(sum_type or received.dtype), axis=1)


def scatter_dir(part, sizes):
    rows, width = part.shape
    size = sizes[0] * sizes[1]
    split = part.reshape(rows, size, width // size)
    received = lax.all_to_all(narrow_rows(split), DIR_AXES, 1, 1, tiled=True)
    return jnp.sum(widen_rows(received), axis=1)


def narrow_rows(part):
    coef_rows = part[: 2 * C].astype(jnp.bfloat16)
    place_high = part[2 * C :].astype(jnp.bfloat16)
    place_low = (part[2 * C :] - place_high.astype(jnp.float32)).astype(jnp.bfloat16)
    return jnp.concatenate([coef_rows, place_high, place_low], axis=0)


def widen_rows(packed):
    wide = packed.astype(jnp.float32)
    place_count = (packed.shape[0] - 2 * C) // 2
    place_rows = wide[2 * C : 2 * C + place_count] + wide[2 * C + place_count :]
    return jnp.concatenate([wide[: 2 * C], place_rows], axis=0)


def body(coefficients, positions, polar, azimuth, weights, farmap, dir_sizes, dom_size):
    own_count = coefficients.shape[2]
    dir_size = dir_sizes[0] * dir_sizes[1]
    own_rows = coefficients.reshape(2 * C, own_count)
    place_high = positions.astype(jnp.bfloat16)
    place_rest = positions - place_high.astype(jnp.float32)
    place_mid = place_rest.astype(jnp.bfloat16)
    place_low = (place_rest - place_mid.astype(jnp.float32)).astype(jnp.bfloat16)
    packed = jnp.concatenate([own_rows, place_high, place_mid, place_low], axis=0)
    packed_blocks = gather_blocks(packed, DIR_AXES, dir_size)
    domain_packed = jnp.moveaxis(packed_blocks, 0, 1).reshape(
        packed.shape[0], dir_size * own_count
    )
    domain_rows = domain_packed[: 2 * C]
    pieces = domain_packed[2 * C :].astype(jnp.float32)
    domain_places = pieces[0:3] + pieces[3:6] + pieces[6:9]
    vectors = unit_vectors(polar, azimuth)
    cos_tile, sin_tile = phase_tile(domain_places, vectors)
    partial_fields = field_terms(domain_rows, cos_tile, sin_tile)
    dir_count = polar.shape[0]
    slice_width = dir_count // dom_size
    fields_slice = scatter_sum(partial_fields.astype(jnp.bfloat16), DOM_AXES, dom_size, jnp.float32)
    offset = lax.axis_index(DOM_AXES) * slice_width
    farmap_slice = lax.dynamic_slice_in_dim(farmap, offset, slice_width, 3)
    weights_slice = lax.dynamic_slice_in_dim(weights, offset, slice_width, 0)
    adjoint_slice = cotangent_rows(fields_slice, farmap_slice, weights_slice)
    adjoint_blocks = gather_blocks(adjoint_slice, DOM_AXES, dom_size)
    adjoint = jnp.moveaxis(adjoint_blocks, 0, 1).reshape(2 * C, dir_count)
    stacked = stacked_rows(adjoint, vectors)
    coef_part, place_part = gradients(adjoint_terms(stacked, cos_tile, sin_tile), domain_rows)
    part = jnp.concatenate([coef_part, place_part], axis=0)
    reduced = scatter_dir(part, dir_sizes)
    return (reduced[: 2 * C].reshape(2, C, own_count), reduced[2 * C :])


def solution(mesh):
    dom_size = mesh.shape["dom"]
    dir_size = mesh.shape["dir"]
    chips_z = 2 if dom_size % 4 == 0 else 1
    dom_sizes = (dom_size // (2 * chips_z), chips_z, 2)
    x_size = 4 if dir_size % 4 == 0 else dir_size
    dir_sizes = (x_size, dir_size // x_size)
    fine = jax.sharding.Mesh(
        mesh.devices.reshape(dom_sizes + dir_sizes), DOM_AXES + DIR_AXES
    )
    every = DOM_AXES + DIR_AXES
    placed = (
        P(None, None, every),
        P(None, every),
        P(DIR_AXES),
        P(DIR_AXES),
        P(DIR_AXES),
        P(None, None, None, DIR_AXES),
    )
    return jax.shard_map(
        functools.partial(body, dir_sizes=dir_sizes, dom_size=dom_size),
        mesh=fine,
        in_specs=placed,
        out_specs=(P(None, None, every), P(None, every)),
        check_vma=False,
    )
```

```python
import functools

import jax
import jax.numpy as jnp
from jax import lax
import numpy as np
from jax.sharding import PartitionSpec as P

C = 70


def unit_vectors(polar, azimuth):
    sine_polar = jnp.sin(polar)
    return jnp.stack([sine_polar * jnp.cos(azimuth), sine_polar * jnp.sin(azimuth), jnp.cos(polar)])


def sine_cosine(angles):
    quarter = jnp.round(angles * np.float32(2.0 / np.pi))
    reduced = angles - quarter * np.float32(1.5703125)
    reduced = reduced - quarter * np.float32(4.837512969970703125e-4)
    reduced = reduced - quarter * np.float32(7.54978995489188216e-8)
    square = reduced * reduced
    sine = reduced + reduced * square * (
        np.float32(-1 / 6)
        + square * (np.float32(1 / 120) + square * (np.float32(-1 / 5040) + square * np.float32(1 / 362880)))
    )
    cosine = np.float32(1) + square * (
        np.float32(-0.5)
        + square * (np.float32(1 / 24) + square * (np.float32(-1 / 720) + square * np.float32(1 / 40320)))
    )
    turn = quarter.astype(jnp.int32)
    odd = (turn & 1) == 1
    cos_base = jnp.where(odd, sine, cosine)
    sin_base = jnp.where(odd, cosine, sine)
    cos_value = jnp.where(((turn + 1) & 2) == 2, -cos_base, cos_base)
    sin_value = jnp.where((turn & 2) == 2, -sin_base, sin_base)
    return (cos_value, sin_value)


def phase_tile(places, vectors):
    angles = (
        places[0][:, None] * vectors[0][None, :]
        + places[1][:, None] * vectors[1][None, :]
        + places[2][:, None] * vectors[2][None, :]
    )
    cos_value, sin_value = sine_cosine(angles)
    return (cos_value.astype(jnp.bfloat16), sin_value.astype(jnp.bfloat16))


def field_terms(coef_block, cos_tile, sin_tile):
    order_count = coef_block.shape[0] // 2
    real_rows = coef_block[:order_count]
    imag_rows = coef_block[order_count:]
    top_rows = jnp.concatenate([real_rows, imag_rows], axis=1)
    low_rows = jnp.concatenate([imag_rows, -real_rows], axis=1)
    left_side = jnp.concatenate([top_rows, low_rows], axis=0)
    right_side = jnp.concatenate([cos_tile, sin_tile], axis=0)
    return jnp.dot(left_side, right_side, preferred_element_type=jnp.float32)


def adjoint_terms(stacked, cos_tile, sin_tile):
    order_count = stacked.shape[0] // 2
    real_rows = stacked[:order_count]
    imag_rows = stacked[order_count:]
    top_rows = jnp.concatenate([real_rows, imag_rows], axis=1)
    low_rows = jnp.concatenate([imag_rows, -real_rows], axis=1)
    left_side = jnp.concatenate([top_rows, low_rows], axis=0)
    right_side = jnp.concatenate([cos_tile, sin_tile], axis=1)
    return lax.dot_general(
        left_side, right_side, (((1,), (1,)), ((), ())), preferred_element_type=jnp.float32
    )


def amplitude_parts(fields, farmap):
    order_count = fields.shape[0] // 2
    field_real = fields[:order_count][None]
    field_imag = fields[order_count:][None]
    map_real = farmap[:, 0]
    map_imag = farmap[:, 1]
    amp_real = jnp.sum(map_real * field_real - map_imag * field_imag, axis=1)
    amp_imag = jnp.sum(map_real * field_imag + map_imag * field_real, axis=1)
    return (amp_real, amp_imag)


def cotangent_from(amp_real, amp_imag, farmap, weights):
    map_real = farmap[:, 0]
    map_imag = farmap[:, 1]
    cot_real = weights * jnp.sum(
        amp_real[:, None] * map_real + amp_imag[:, None] * map_imag, axis=0
    )
    cot_imag = weights * jnp.sum(
        amp_real[:, None] * map_imag - amp_imag[:, None] * map_real, axis=0
    )
    return jnp.concatenate([cot_real, cot_imag], axis=0).astype(jnp.bfloat16)


def cotangent_rows(fields, farmap, weights):
    amp_real, amp_imag = amplitude_parts(fields, farmap)
    return cotangent_from(amp_real, amp_imag, farmap, weights)


def stacked_rows(adjoint, vectors):
    order_count = adjoint.shape[0] // 2
    widened = adjoint.astype(jnp.float32)
    scaled = [(vectors[axis_id][None, :] * widened).astype(jnp.bfloat16) for axis_id in range(3)]
    real_parts = [adjoint[:order_count]] + [item[:order_count] for item in scaled]
    imag_parts = [adjoint[order_count:]] + [item[order_count:] for item in scaled]
    return jnp.concatenate(real_parts + imag_parts, axis=0)


def gradients(output, coef_block):
    order_count = coef_block.shape[0] // 2
    real_out = output[: 4 * order_count]
    imag_out = output[4 * order_count :]
    coef_term = jnp.concatenate(
        [2.0 * real_out[:order_count], -2.0 * imag_out[:order_count]], axis=0
    )
    coef_real = coef_block[:order_count].astype(jnp.float32)
    coef_imag = coef_block[order_count:].astype(jnp.float32)
    place_terms = []
    for axis_id in range(3):
        lower_row = (axis_id + 1) * order_count
        upper_row = (axis_id + 2) * order_count
        place_terms.append(
            2.0
            * jnp.sum(
                coef_real * imag_out[lower_row:upper_row]
                + coef_imag * real_out[lower_row:upper_row],
                axis=0,
            )
        )
    return (coef_term, jnp.stack(place_terms))


DOM_AXES = ("y", "z_lo", "core")
DIR_AXES = ("x", "z_hi")


def gather_blocks(block, axis_name, size):
    spread = jnp.broadcast_to(block[None], (size,) + block.shape)
    return lax.all_to_all(spread, axis_name, 0, 0, tiled=True)


def scatter_sum(part, axis_name, size, sum_type=None):
    rows, width = part.shape
    split = part.reshape(rows, size, width // size)
    received = lax.all_to_all(split, axis_name, 1, 1, tiled=True)
    return jnp.sum(received.astype(sum_type or received.dtype), axis=1)


def scatter_dir(part, sizes):
    rows, width = part.shape
    split = part.reshape(rows, sizes[0], sizes[1] * width // (sizes[0] * sizes[1]))
    outer = jnp.sum(lax.all_to_all(split, DIR_AXES[0], 1, 1, tiled=True), axis=1)
    return scatter_sum(outer, DIR_AXES[1], sizes[1])


def body(coefficients, positions, polar, azimuth, weights, farmap, dir_sizes, dom_size):
    own_count = coefficients.shape[2]
    dir_size = dir_sizes[0] * dir_sizes[1]
    own_rows = coefficients.reshape(2 * C, own_count)
    place_high = positions.astype(jnp.bfloat16)
    place_rest = positions - place_high.astype(jnp.float32)
    place_mid = place_rest.astype(jnp.bfloat16)
    place_low = (place_rest - place_mid.astype(jnp.float32)).astype(jnp.bfloat16)
    packed = jnp.concatenate([own_rows, place_high, place_mid, place_low], axis=0)
    packed_blocks = gather_blocks(packed, DIR_AXES, dir_size)
    domain_packed = jnp.moveaxis(packed_blocks, 0, 1).reshape(
        packed.shape[0], dir_size * own_count
    )
    domain_rows = domain_packed[: 2 * C]
    pieces = domain_packed[2 * C :].astype(jnp.float32)
    domain_places = pieces[0:3] + pieces[3:6] + pieces[6:9]
    vectors = unit_vectors(polar, azimuth)
    cos_tile, sin_tile = phase_tile(domain_places, vectors)
    partial_fields = field_terms(domain_rows, cos_tile, sin_tile)
    dir_count = polar.shape[0]
    slice_width = dir_count // dom_size
    fields_slice = scatter_sum(partial_fields, DOM_AXES, dom_size)
    offset = lax.axis_index(DOM_AXES) * slice_width
    farmap_slice = lax.dynamic_slice_in_dim(farmap, offset, slice_width, 3)
    weights_slice = lax.dynamic_slice_in_dim(weights, offset, slice_width, 0)
    adjoint_slice = cotangent_rows(fields_slice, farmap_slice, weights_slice)
    adjoint_blocks = gather_blocks(adjoint_slice, DOM_AXES, dom_size)
    adjoint = jnp.moveaxis(adjoint_blocks, 0, 1).reshape(2 * C, dir_count)
    stacked = stacked_rows(adjoint, vectors)
    coef_part, place_part = gradients(adjoint_terms(stacked, cos_tile, sin_tile), domain_rows)
    part = jnp.concatenate([coef_part, place_part], axis=0)
    reduced = scatter_dir(part, dir_sizes)
    return (reduced[: 2 * C].reshape(2, C, own_count), reduced[2 * C :])


def solution(mesh):
    dom_size = mesh.shape["dom"]
    dir_size = mesh.shape["dir"]
    chips_z = 2 if dom_size % 4 == 0 else 1
    dom_sizes = (dom_size // (2 * chips_z), chips_z, 2)
    x_size = 4 if dir_size % 4 == 0 else dir_size
    dir_sizes = (x_size, dir_size // x_size)
    fine = jax.sharding.Mesh(
        mesh.devices.reshape(dom_sizes + dir_sizes), DOM_AXES + DIR_AXES
    )
    every = DOM_AXES + DIR_AXES
    placed = (
        P(None, None, every),
        P(None, every),
        P(DIR_AXES),
        P(DIR_AXES),
        P(DIR_AXES),
        P(None, None, None, DIR_AXES),
    )
    return jax.shard_map(
        functools.partial(body, dir_sizes=dir_sizes, dom_size=dom_size),
        mesh=fine,
        in_specs=placed,
        out_specs=(P(None, None, every), P(None, every)),
        check_vma=False,
    )
```

```python
import functools

import jax
import jax.numpy as jnp
from jax import lax
import numpy as np
from jax.sharding import PartitionSpec as P

C = 70


def unit_vectors(polar, azimuth):
    sine_polar = jnp.sin(polar)
    return jnp.stack([sine_polar * jnp.cos(azimuth), sine_polar * jnp.sin(azimuth), jnp.cos(polar)])


def sine_cosine(angles):
    quarter = jnp.round(angles * np.float32(2.0 / np.pi))
    reduced = angles - quarter * np.float32(1.5703125)
    reduced = reduced - quarter * np.float32(4.837512969970703125e-4)
    reduced = reduced - quarter * np.float32(7.54978995489188216e-8)
    square = reduced * reduced
    sine = reduced + reduced * square * (
        np.float32(-1 / 6)
        + square * (np.float32(1 / 120) + square * (np.float32(-1 / 5040) + square * np.float32(1 / 362880)))
    )
    cosine = np.float32(1) + square * (
        np.float32(-0.5)
        + square * (np.float32(1 / 24) + square * (np.float32(-1 / 720) + square * np.float32(1 / 40320)))
    )
    turn = quarter.astype(jnp.int32)
    odd = (turn & 1) == 1
    cos_base = jnp.where(odd, sine, cosine)
    sin_base = jnp.where(odd, cosine, sine)
    cos_value = jnp.where(((turn + 1) & 2) == 2, -cos_base, cos_base)
    sin_value = jnp.where((turn & 2) == 2, -sin_base, sin_base)
    return (cos_value, sin_value)


def phase_tile(places, vectors):
    angles = (
        places[0][:, None] * vectors[0][None, :]
        + places[1][:, None] * vectors[1][None, :]
        + places[2][:, None] * vectors[2][None, :]
    )
    cos_value, sin_value = sine_cosine(angles)
    return (cos_value.astype(jnp.bfloat16), sin_value.astype(jnp.bfloat16))


def field_terms(coef_block, cos_tile, sin_tile):
    order_count = coef_block.shape[0] // 2
    real_rows = coef_block[:order_count]
    imag_rows = coef_block[order_count:]
    top_rows = jnp.concatenate([real_rows, imag_rows], axis=1)
    low_rows = jnp.concatenate([imag_rows, -real_rows], axis=1)
    left_side = jnp.concatenate([top_rows, low_rows], axis=0)
    right_side = jnp.concatenate([cos_tile, sin_tile], axis=0)
    return jnp.dot(left_side, right_side, preferred_element_type=jnp.float32)


def adjoint_terms(stacked, cos_tile, sin_tile):
    order_count = stacked.shape[0] // 2
    real_rows = stacked[:order_count]
    imag_rows = stacked[order_count:]
    top_rows = jnp.concatenate([real_rows, imag_rows], axis=1)
    low_rows = jnp.concatenate([imag_rows, -real_rows], axis=1)
    left_side = jnp.concatenate([top_rows, low_rows], axis=0)
    right_side = jnp.concatenate([cos_tile, sin_tile], axis=1)
    return lax.dot_general(
        left_side, right_side, (((1,), (1,)), ((), ())), preferred_element_type=jnp.float32
    )


def amplitude_parts(fields, farmap):
    order_count = fields.shape[0] // 2
    field_real = fields[:order_count][None]
    field_imag = fields[order_count:][None]
    map_real = farmap[:, 0]
    map_imag = farmap[:, 1]
    amp_real = jnp.sum(map_real * field_real - map_imag * field_imag, axis=1)
    amp_imag = jnp.sum(map_real * field_imag + map_imag * field_real, axis=1)
    return (amp_real, amp_imag)


def cotangent_from(amp_real, amp_imag, farmap, weights):
    map_real = farmap[:, 0]
    map_imag = farmap[:, 1]
    cot_real = weights * jnp.sum(
        amp_real[:, None] * map_real + amp_imag[:, None] * map_imag, axis=0
    )
    cot_imag = weights * jnp.sum(
        amp_real[:, None] * map_imag - amp_imag[:, None] * map_real, axis=0
    )
    return jnp.concatenate([cot_real, cot_imag], axis=0).astype(jnp.bfloat16)


def cotangent_rows(fields, farmap, weights):
    amp_real, amp_imag = amplitude_parts(fields, farmap)
    return cotangent_from(amp_real, amp_imag, farmap, weights)


def stacked_rows(adjoint, vectors):
    order_count = adjoint.shape[0] // 2
    widened = adjoint.astype(jnp.float32)
    scaled = [(vectors[axis_id][None, :] * widened).astype(jnp.bfloat16) for axis_id in range(3)]
    real_parts = [adjoint[:order_count]] + [item[:order_count] for item in scaled]
    imag_parts = [adjoint[order_count:]] + [item[order_count:] for item in scaled]
    return jnp.concatenate(real_parts + imag_parts, axis=0)


def gradients(output, coef_block):
    order_count = coef_block.shape[0] // 2
    real_out = output[: 4 * order_count]
    imag_out = output[4 * order_count :]
    coef_term = jnp.concatenate(
        [2.0 * real_out[:order_count], -2.0 * imag_out[:order_count]], axis=0
    )
    coef_real = coef_block[:order_count].astype(jnp.float32)
    coef_imag = coef_block[order_count:].astype(jnp.float32)
    place_terms = []
    for axis_id in range(3):
        lower_row = (axis_id + 1) * order_count
        upper_row = (axis_id + 2) * order_count
        place_terms.append(
            2.0
            * jnp.sum(
                coef_real * imag_out[lower_row:upper_row]
                + coef_imag * real_out[lower_row:upper_row],
                axis=0,
            )
        )
    return (coef_term, jnp.stack(place_terms))


DOM_AXES = ("y", "z_lo", "core")
DIR_AXES = ("x", "z_hi")


def gather_blocks(block, axis_name, size):
    spread = jnp.broadcast_to(block[None], (size,) + block.shape)
    return lax.all_to_all(spread, axis_name, 0, 0, tiled=True)


def scatter_sum(part, axis_name, size, sum_type=None):
    rows, width = part.shape
    split = part.reshape(rows, size, width // size)
    received = lax.all_to_all(split, axis_name, 1, 1, tiled=True)
    return jnp.sum(received.astype(sum_type or received.dtype), axis=1)


def scatter_dir(part, sizes):
    rows, width = part.shape
    size = sizes[0] * sizes[1]
    split = part.reshape(rows, size, width // size)
    received = lax.all_to_all(narrow_rows(split), DIR_AXES, 1, 1, tiled=True)
    return jnp.sum(widen_rows(received), axis=1)


def narrow_rows(part):
    coef_rows = part[: 2 * C].astype(jnp.bfloat16)
    place_high = part[2 * C :].astype(jnp.bfloat16)
    place_low = (part[2 * C :] - place_high.astype(jnp.float32)).astype(jnp.bfloat16)
    return jnp.concatenate([coef_rows, place_high, place_low], axis=0)


def widen_rows(packed):
    wide = packed.astype(jnp.float32)
    place_count = (packed.shape[0] - 2 * C) // 2
    place_rows = wide[2 * C : 2 * C + place_count] + wide[2 * C + place_count :]
    return jnp.concatenate([wide[: 2 * C], place_rows], axis=0)


def body(coefficients, positions, polar, azimuth, weights, farmap, dir_sizes, dom_size):
    own_count = coefficients.shape[2]
    dir_size = dir_sizes[0] * dir_sizes[1]
    own_rows = coefficients.reshape(2 * C, own_count)
    place_high = positions.astype(jnp.bfloat16)
    place_rest = positions - place_high.astype(jnp.float32)
    place_mid = place_rest.astype(jnp.bfloat16)
    place_low = (place_rest - place_mid.astype(jnp.float32)).astype(jnp.bfloat16)
    packed = jnp.concatenate([own_rows, place_high, place_mid, place_low], axis=0)
    packed_blocks = gather_blocks(packed, DOM_AXES, dom_size)
    domain_packed = jnp.moveaxis(packed_blocks, 0, 1).reshape(
        packed.shape[0], dom_size * own_count
    )
    domain_rows = domain_packed[: 2 * C]
    pieces = domain_packed[2 * C :].astype(jnp.float32)
    domain_places = pieces[0:3] + pieces[3:6] + pieces[6:9]
    slice_width = polar.shape[0] // dom_size
    offset = lax.axis_index(DOM_AXES) * slice_width
    own_angles = lax.dynamic_slice_in_dim(jnp.stack([polar, azimuth]), offset, slice_width, 1)
    angle_blocks = gather_blocks(own_angles, DIR_AXES, dir_size)
    set_angles = jnp.moveaxis(angle_blocks, 0, 1).reshape(2, dir_size * slice_width)
    vectors = unit_vectors(set_angles[0], set_angles[1])
    cos_tile, sin_tile = phase_tile(domain_places, vectors)
    partial_fields = field_terms(domain_rows, cos_tile, sin_tile)
    fields_slice = scatter_sum(partial_fields.astype(jnp.bfloat16), DIR_AXES, dir_size, jnp.float32)
    farmap_slice = lax.dynamic_slice_in_dim(farmap, offset, slice_width, 3)
    weights_slice = lax.dynamic_slice_in_dim(weights, offset, slice_width, 0)
    adjoint_slice = cotangent_rows(fields_slice, farmap_slice, weights_slice)
    adjoint_blocks = gather_blocks(adjoint_slice, DIR_AXES, dir_size)
    adjoint = jnp.moveaxis(adjoint_blocks, 0, 1).reshape(2 * C, dir_size * slice_width)
    stacked = stacked_rows(adjoint, vectors)
    coef_part, place_part = gradients(adjoint_terms(stacked, cos_tile, sin_tile), domain_rows)
    part = jnp.concatenate([coef_part, place_part], axis=0)
    rows, width = part.shape
    split = part.reshape(rows, dom_size, width // dom_size)
    received = lax.all_to_all(narrow_rows(split), DOM_AXES, 1, 1, tiled=True)
    reduced = jnp.sum(widen_rows(received), axis=1)
    return (reduced[: 2 * C].reshape(2, C, own_count), reduced[2 * C :])


def solution(mesh):
    dom_size = mesh.shape["dom"]
    dir_size = mesh.shape["dir"]
    chips_z = 2 if dom_size % 4 == 0 else 1
    dom_sizes = (dom_size // (2 * chips_z), chips_z, 2)
    x_size = 4 if dir_size % 4 == 0 else dir_size
    dir_sizes = (x_size, dir_size // x_size)
    fine = jax.sharding.Mesh(
        mesh.devices.reshape(dom_sizes + dir_sizes), DOM_AXES + DIR_AXES
    )
    every = DOM_AXES + DIR_AXES
    placed = (
        P(None, None, every),
        P(None, every),
        P(DIR_AXES),
        P(DIR_AXES),
        P(DIR_AXES),
        P(None, None, None, DIR_AXES),
    )
    return jax.shard_map(
        functools.partial(body, dir_sizes=dir_sizes, dom_size=dom_size),
        mesh=fine,
        in_specs=placed,
        out_specs=(P(None, None, every), P(None, every)),
        check_vma=False,
    )
```

```python
import functools

import jax
import jax.numpy as jnp
from jax import lax
import numpy as np
from jax.sharding import PartitionSpec as P

C = 70


def unit_vectors(polar, azimuth):
    sine_polar = jnp.sin(polar)
    return jnp.stack([sine_polar * jnp.cos(azimuth), sine_polar * jnp.sin(azimuth), jnp.cos(polar)])


def sine_cosine(angles):
    quarter = jnp.round(angles * np.float32(2.0 / np.pi))
    reduced = angles - quarter * np.float32(1.5703125)
    reduced = reduced - quarter * np.float32(4.837512969970703125e-4)
    reduced = reduced - quarter * np.float32(7.54978995489188216e-8)
    square = reduced * reduced
    sine = reduced + reduced * square * (
        np.float32(-1 / 6)
        + square * (np.float32(1 / 120) + square * (np.float32(-1 / 5040) + square * np.float32(1 / 362880)))
    )
    cosine = np.float32(1) + square * (
        np.float32(-0.5)
        + square * (np.float32(1 / 24) + square * (np.float32(-1 / 720) + square * np.float32(1 / 40320)))
    )
    turn = quarter.astype(jnp.int32)
    odd = (turn & 1) == 1
    cos_base = jnp.where(odd, sine, cosine)
    sin_base = jnp.where(odd, cosine, sine)
    cos_value = jnp.where(((turn + 1) & 2) == 2, -cos_base, cos_base)
    sin_value = jnp.where((turn & 2) == 2, -sin_base, sin_base)
    return (cos_value, sin_value)


def phase_tile(places, vectors):
    angles = (
        places[0][:, None] * vectors[0][None, :]
        + places[1][:, None] * vectors[1][None, :]
        + places[2][:, None] * vectors[2][None, :]
    )
    cos_value, sin_value = sine_cosine(angles)
    return (cos_value.astype(jnp.bfloat16), sin_value.astype(jnp.bfloat16))


def field_terms(coef_block, cos_tile, sin_tile):
    order_count = coef_block.shape[0] // 2
    real_rows = coef_block[:order_count]
    imag_rows = coef_block[order_count:]
    top_rows = jnp.concatenate([real_rows, imag_rows], axis=1)
    low_rows = jnp.concatenate([imag_rows, -real_rows], axis=1)
    left_side = jnp.concatenate([top_rows, low_rows], axis=0)
    right_side = jnp.concatenate([cos_tile, sin_tile], axis=0)
    return jnp.dot(left_side, right_side, preferred_element_type=jnp.float32)


def adjoint_terms(stacked, cos_tile, sin_tile):
    order_count = stacked.shape[0] // 2
    real_rows = stacked[:order_count]
    imag_rows = stacked[order_count:]
    top_rows = jnp.concatenate([real_rows, imag_rows], axis=1)
    low_rows = jnp.concatenate([imag_rows, -real_rows], axis=1)
    left_side = jnp.concatenate([top_rows, low_rows], axis=0)
    right_side = jnp.concatenate([cos_tile, sin_tile], axis=1)
    return lax.dot_general(
        left_side, right_side, (((1,), (1,)), ((), ())), preferred_element_type=jnp.float32
    )


def amplitude_parts(fields, farmap):
    order_count = fields.shape[0] // 2
    field_real = fields[:order_count][None]
    field_imag = fields[order_count:][None]
    map_real = farmap[:, 0]
    map_imag = farmap[:, 1]
    amp_real = jnp.sum(map_real * field_real - map_imag * field_imag, axis=1)
    amp_imag = jnp.sum(map_real * field_imag + map_imag * field_real, axis=1)
    return (amp_real, amp_imag)


def cotangent_from(amp_real, amp_imag, farmap, weights):
    map_real = farmap[:, 0]
    map_imag = farmap[:, 1]
    cot_real = weights * jnp.sum(
        amp_real[:, None] * map_real + amp_imag[:, None] * map_imag, axis=0
    )
    cot_imag = weights * jnp.sum(
        amp_real[:, None] * map_imag - amp_imag[:, None] * map_real, axis=0
    )
    return jnp.concatenate([cot_real, cot_imag], axis=0).astype(jnp.bfloat16)


def cotangent_rows(fields, farmap, weights):
    amp_real, amp_imag = amplitude_parts(fields, farmap)
    return cotangent_from(amp_real, amp_imag, farmap, weights)


def stacked_rows(adjoint, vectors):
    order_count = adjoint.shape[0] // 2
    widened = adjoint.astype(jnp.float32)
    scaled = [(vectors[axis_id][None, :] * widened).astype(jnp.bfloat16) for axis_id in range(3)]
    real_parts = [adjoint[:order_count]] + [item[:order_count] for item in scaled]
    imag_parts = [adjoint[order_count:]] + [item[order_count:] for item in scaled]
    return jnp.concatenate(real_parts + imag_parts, axis=0)


def gradients(output, coef_block):
    order_count = coef_block.shape[0] // 2
    real_out = output[: 4 * order_count]
    imag_out = output[4 * order_count :]
    coef_term = jnp.concatenate(
        [2.0 * real_out[:order_count], -2.0 * imag_out[:order_count]], axis=0
    )
    coef_real = coef_block[:order_count].astype(jnp.float32)
    coef_imag = coef_block[order_count:].astype(jnp.float32)
    place_terms = []
    for axis_id in range(3):
        lower_row = (axis_id + 1) * order_count
        upper_row = (axis_id + 2) * order_count
        place_terms.append(
            2.0
            * jnp.sum(
                coef_real * imag_out[lower_row:upper_row]
                + coef_imag * real_out[lower_row:upper_row],
                axis=0,
            )
        )
    return (coef_term, jnp.stack(place_terms))


DOM_AXES = ("y", "z_lo", "core")
DIR_AXES = ("x", "z_hi")


def gather_blocks(block, axis_name, size):
    spread = jnp.broadcast_to(block[None], (size,) + block.shape)
    return lax.all_to_all(spread, axis_name, 0, 0, tiled=True)


def scatter_sum(part, axis_name, size, sum_type=None):
    rows, width = part.shape
    split = part.reshape(rows, size, width // size)
    received = lax.all_to_all(split, axis_name, 1, 1, tiled=True)
    return jnp.sum(received.astype(sum_type or received.dtype), axis=1)


def scatter_dir(part, sizes):
    rows, width = part.shape
    size = sizes[0] * sizes[1]
    split = part.reshape(rows, size, width // size)
    received = lax.all_to_all(narrow_rows(split), DIR_AXES, 1, 1, tiled=True)
    return jnp.sum(widen_rows(received), axis=1)


def narrow_rows(part):
    coef_rows = part[: 2 * C].astype(jnp.bfloat16)
    place_high = part[2 * C :].astype(jnp.bfloat16)
    place_low = (part[2 * C :] - place_high.astype(jnp.float32)).astype(jnp.bfloat16)
    return jnp.concatenate([coef_rows, place_high, place_low], axis=0)


def widen_rows(packed):
    wide = packed.astype(jnp.float32)
    place_count = (packed.shape[0] - 2 * C) // 2
    place_rows = wide[2 * C : 2 * C + place_count] + wide[2 * C + place_count :]
    return jnp.concatenate([wide[: 2 * C], place_rows], axis=0)


def body(coefficients, positions, polar, azimuth, weights, farmap, dir_sizes, dom_size):
    own_count = coefficients.shape[2]
    dir_size = dir_sizes[0] * dir_sizes[1]
    own_rows = coefficients.reshape(2 * C, own_count)
    place_high = positions.astype(jnp.bfloat16)
    place_rest = positions - place_high.astype(jnp.float32)
    place_mid = place_rest.astype(jnp.bfloat16)
    place_low = (place_rest - place_mid.astype(jnp.float32)).astype(jnp.bfloat16)
    packed = jnp.concatenate([own_rows, place_high, place_mid, place_low], axis=0)
    packed_blocks = gather_blocks(packed, DIR_AXES, dir_size)
    domain_packed = jnp.moveaxis(packed_blocks, 0, 1).reshape(
        packed.shape[0], dir_size * own_count
    )
    domain_rows = domain_packed[: 2 * C]
    pieces = domain_packed[2 * C :].astype(jnp.float32)
    domain_places = pieces[0:3] + pieces[3:6] + pieces[6:9]
    vectors = unit_vectors(polar, azimuth)
    cos_tile, sin_tile = phase_tile(domain_places, vectors)
    partial_fields = field_terms(domain_rows, cos_tile, sin_tile)
    amp_real, amp_imag = amplitude_parts(partial_fields, farmap)
    amp_parts = gather_blocks(jnp.stack([amp_real, amp_imag]), DOM_AXES, dom_size)
    amp_total = jnp.sum(amp_parts, axis=0)
    adjoint = cotangent_from(amp_total[0], amp_total[1], farmap, weights)
    stacked = stacked_rows(adjoint, vectors)
    coef_part, place_part = gradients(adjoint_terms(stacked, cos_tile, sin_tile), domain_rows)
    part = jnp.concatenate([coef_part, place_part], axis=0)
    reduced = scatter_dir(part, dir_sizes)
    return (reduced[: 2 * C].reshape(2, C, own_count), reduced[2 * C :])


def solution(mesh):
    dom_size = mesh.shape["dom"]
    dir_size = mesh.shape["dir"]
    chips_z = 2 if dom_size % 4 == 0 else 1
    dom_sizes = (dom_size // (2 * chips_z), chips_z, 2)
    x_size = 4 if dir_size % 4 == 0 else dir_size
    dir_sizes = (x_size, dir_size // x_size)
    fine = jax.sharding.Mesh(
        mesh.devices.reshape(dom_sizes + dir_sizes), DOM_AXES + DIR_AXES
    )
    every = DOM_AXES + DIR_AXES
    placed = (
        P(None, None, every),
        P(None, every),
        P(DIR_AXES),
        P(DIR_AXES),
        P(DIR_AXES),
        P(None, None, None, DIR_AXES),
    )
    return jax.shard_map(
        functools.partial(body, dir_sizes=dir_sizes, dom_size=dom_size),
        mesh=fine,
        in_specs=placed,
        out_specs=(P(None, None, every), P(None, every)),
        check_vma=False,
    )
```

```python
import functools

import jax
import jax.numpy as jnp
from jax import lax
import numpy as np
from jax.sharding import PartitionSpec as P

C = 70


def unit_vectors(polar, azimuth):
    sine_polar = jnp.sin(polar)
    return jnp.stack([sine_polar * jnp.cos(azimuth), sine_polar * jnp.sin(azimuth), jnp.cos(polar)])


def sine_cosine(angles):
    quarter = jnp.round(angles * np.float32(2.0 / np.pi))
    reduced = angles - quarter * np.float32(1.5703125)
    reduced = reduced - quarter * np.float32(4.837512969970703125e-4)
    reduced = reduced - quarter * np.float32(7.54978995489188216e-8)
    square = reduced * reduced
    sine = reduced + reduced * square * (
        np.float32(-1 / 6)
        + square * (np.float32(1 / 120) + square * (np.float32(-1 / 5040) + square * np.float32(1 / 362880)))
    )
    cosine = np.float32(1) + square * (
        np.float32(-0.5)
        + square * (np.float32(1 / 24) + square * (np.float32(-1 / 720) + square * np.float32(1 / 40320)))
    )
    turn = quarter.astype(jnp.int32)
    odd = (turn & 1) == 1
    cos_base = jnp.where(odd, sine, cosine)
    sin_base = jnp.where(odd, cosine, sine)
    cos_value = jnp.where(((turn + 1) & 2) == 2, -cos_base, cos_base)
    sin_value = jnp.where((turn & 2) == 2, -sin_base, sin_base)
    return (cos_value, sin_value)


def phase_tile(places, vectors):
    angles = (
        places[0][:, None] * vectors[0][None, :]
        + places[1][:, None] * vectors[1][None, :]
        + places[2][:, None] * vectors[2][None, :]
    )
    cos_value, sin_value = sine_cosine(angles)
    return (cos_value.astype(jnp.bfloat16), sin_value.astype(jnp.bfloat16))


def field_terms(coef_block, cos_tile, sin_tile):
    order_count = coef_block.shape[0] // 2
    real_rows = coef_block[:order_count]
    imag_rows = coef_block[order_count:]
    top_rows = jnp.concatenate([real_rows, imag_rows], axis=1)
    low_rows = jnp.concatenate([imag_rows, -real_rows], axis=1)
    left_side = jnp.concatenate([top_rows, low_rows], axis=0)
    right_side = jnp.concatenate([cos_tile, sin_tile], axis=0)
    return jnp.dot(left_side, right_side, preferred_element_type=jnp.float32)


def adjoint_terms(stacked, cos_tile, sin_tile):
    order_count = stacked.shape[0] // 2
    real_rows = stacked[:order_count]
    imag_rows = stacked[order_count:]
    top_rows = jnp.concatenate([real_rows, imag_rows], axis=1)
    low_rows = jnp.concatenate([imag_rows, -real_rows], axis=1)
    left_side = jnp.concatenate([top_rows, low_rows], axis=0)
    right_side = jnp.concatenate([cos_tile, sin_tile], axis=1)
    return lax.dot_general(
        left_side, right_side, (((1,), (1,)), ((), ())), preferred_element_type=jnp.float32
    )


def amplitude_parts(fields, farmap):
    order_count = fields.shape[0] // 2
    field_real = fields[:order_count][None]
    field_imag = fields[order_count:][None]
    map_real = farmap[:, 0]
    map_imag = farmap[:, 1]
    amp_real = jnp.sum(map_real * field_real - map_imag * field_imag, axis=1)
    amp_imag = jnp.sum(map_real * field_imag + map_imag * field_real, axis=1)
    return (amp_real, amp_imag)


def cotangent_from(amp_real, amp_imag, farmap, weights):
    map_real = farmap[:, 0]
    map_imag = farmap[:, 1]
    cot_real = weights * jnp.sum(
        amp_real[:, None] * map_real + amp_imag[:, None] * map_imag, axis=0
    )
    cot_imag = weights * jnp.sum(
        amp_real[:, None] * map_imag - amp_imag[:, None] * map_real, axis=0
    )
    return jnp.concatenate([cot_real, cot_imag], axis=0).astype(jnp.bfloat16)


def cotangent_rows(fields, farmap, weights):
    amp_real, amp_imag = amplitude_parts(fields, farmap)
    return cotangent_from(amp_real, amp_imag, farmap, weights)


def stacked_rows(adjoint, vectors):
    order_count = adjoint.shape[0] // 2
    widened = adjoint.astype(jnp.float32)
    scaled = [(vectors[axis_id][None, :] * widened).astype(jnp.bfloat16) for axis_id in range(3)]
    real_parts = [adjoint[:order_count]] + [item[:order_count] for item in scaled]
    imag_parts = [adjoint[order_count:]] + [item[order_count:] for item in scaled]
    return jnp.concatenate(real_parts + imag_parts, axis=0)


def gradients(output, coef_block):
    order_count = coef_block.shape[0] // 2
    real_out = output[: 4 * order_count]
    imag_out = output[4 * order_count :]
    coef_term = jnp.concatenate(
        [2.0 * real_out[:order_count], -2.0 * imag_out[:order_count]], axis=0
    )
    coef_real = coef_block[:order_count].astype(jnp.float32)
    coef_imag = coef_block[order_count:].astype(jnp.float32)
    place_terms = []
    for axis_id in range(3):
        lower_row = (axis_id + 1) * order_count
        upper_row = (axis_id + 2) * order_count
        place_terms.append(
            2.0
            * jnp.sum(
                coef_real * imag_out[lower_row:upper_row]
                + coef_imag * real_out[lower_row:upper_row],
                axis=0,
            )
        )
    return (coef_term, jnp.stack(place_terms))


DOM_AXES = ("y", "z_lo", "core")
DIR_AXES = ("x", "z_hi")


def gather_blocks(block, axis_name, size):
    spread = jnp.broadcast_to(block[None], (size,) + block.shape)
    return lax.all_to_all(spread, axis_name, 0, 0, tiled=True)


def scatter_sum(part, axis_name, size, sum_type=None):
    rows, width = part.shape
    split = part.reshape(rows, size, width // size)
    received = lax.all_to_all(split, axis_name, 1, 1, tiled=True)
    return jnp.sum(received.astype(sum_type or received.dtype), axis=1)


def scatter_dir(part, sizes):
    rows, width = part.shape
    split = part.reshape(rows, sizes[0], sizes[1] * width // (sizes[0] * sizes[1]))
    outer = jnp.sum(lax.all_to_all(split, DIR_AXES[0], 1, 1, tiled=True), axis=1)
    return scatter_sum(outer, DIR_AXES[1], sizes[1])


def narrow_rows(part):
    coef_rows = part[: 2 * C].astype(jnp.bfloat16)
    place_high = part[2 * C :].astype(jnp.bfloat16)
    place_low = (part[2 * C :] - place_high.astype(jnp.float32)).astype(jnp.bfloat16)
    return jnp.concatenate([coef_rows, place_high, place_low], axis=0)


def widen_rows(packed):
    wide = packed.astype(jnp.float32)
    place_count = (packed.shape[0] - 2 * C) // 2
    place_rows = wide[2 * C : 2 * C + place_count] + wide[2 * C + place_count :]
    return jnp.concatenate([wide[: 2 * C], place_rows], axis=0)


def body(coefficients, positions, polar, azimuth, weights, farmap, dir_sizes, dom_size):
    own_count = coefficients.shape[2]
    dir_size = dir_sizes[0] * dir_sizes[1]
    own_rows = coefficients.reshape(2 * C, own_count)
    place_high = positions.astype(jnp.bfloat16)
    place_rest = positions - place_high.astype(jnp.float32)
    place_mid = place_rest.astype(jnp.bfloat16)
    place_low = (place_rest - place_mid.astype(jnp.float32)).astype(jnp.bfloat16)
    packed = jnp.concatenate([own_rows, place_high, place_mid, place_low], axis=0)
    packed_blocks = gather_blocks(packed, DIR_AXES, dir_size)
    domain_packed = jnp.moveaxis(packed_blocks, 0, 1).reshape(
        packed.shape[0], dir_size * own_count
    )
    domain_rows = domain_packed[: 2 * C]
    pieces = domain_packed[2 * C :].astype(jnp.float32)
    domain_places = pieces[0:3] + pieces[3:6] + pieces[6:9]
    vectors = unit_vectors(polar, azimuth)
    cos_tile, sin_tile = phase_tile(domain_places, vectors)
    partial_fields = field_terms(domain_rows, cos_tile, sin_tile)
    amp_real, amp_imag = amplitude_parts(partial_fields, farmap)
    amp_parts = gather_blocks(jnp.stack([amp_real, amp_imag]), DOM_AXES, dom_size)
    amp_total = jnp.sum(amp_parts, axis=0)
    adjoint = cotangent_from(amp_total[0], amp_total[1], farmap, weights)
    stacked = stacked_rows(adjoint, vectors)
    coef_part, place_part = gradients(adjoint_terms(stacked, cos_tile, sin_tile), domain_rows)
    part = jnp.concatenate([coef_part, place_part], axis=0)
    reduced = scatter_dir(part, dir_sizes)
    return (reduced[: 2 * C].reshape(2, C, own_count), reduced[2 * C :])


def solution(mesh):
    dom_size = mesh.shape["dom"]
    dir_size = mesh.shape["dir"]
    chips_z = 2 if dom_size % 4 == 0 else 1
    dom_sizes = (dom_size // (2 * chips_z), chips_z, 2)
    x_size = 4 if dir_size % 4 == 0 else dir_size
    dir_sizes = (x_size, dir_size // x_size)
    fine = jax.sharding.Mesh(
        mesh.devices.reshape(dom_sizes + dir_sizes), DOM_AXES + DIR_AXES
    )
    every = DOM_AXES + DIR_AXES
    placed = (
        P(None, None, every),
        P(None, every),
        P(DIR_AXES),
        P(DIR_AXES),
        P(DIR_AXES),
        P(None, None, None, DIR_AXES),
    )
    return jax.shard_map(
        functools.partial(body, dir_sizes=dir_sizes, dom_size=dom_size),
        mesh=fine,
        in_specs=placed,
        out_specs=(P(None, None, every), P(None, every)),
        check_vma=False,
    )
```

```python
import functools

import jax
import jax.numpy as jnp
from jax import lax
import numpy as np
from jax.sharding import PartitionSpec as P

C = 70


def unit_vectors(polar, azimuth):
    sine_polar = jnp.sin(polar)
    return jnp.stack([sine_polar * jnp.cos(azimuth), sine_polar * jnp.sin(azimuth), jnp.cos(polar)])


def sine_cosine(angles):
    quarter = jnp.round(angles * np.float32(2.0 / np.pi))
    reduced = angles - quarter * np.float32(1.5703125)
    reduced = reduced - quarter * np.float32(4.837512969970703125e-4)
    reduced = reduced - quarter * np.float32(7.54978995489188216e-8)
    square = reduced * reduced
    sine = reduced + reduced * square * (
        np.float32(-1 / 6)
        + square * (np.float32(1 / 120) + square * (np.float32(-1 / 5040) + square * np.float32(1 / 362880)))
    )
    cosine = np.float32(1) + square * (
        np.float32(-0.5)
        + square * (np.float32(1 / 24) + square * (np.float32(-1 / 720) + square * np.float32(1 / 40320)))
    )
    turn = quarter.astype(jnp.int32)
    odd = (turn & 1) == 1
    cos_base = jnp.where(odd, sine, cosine)
    sin_base = jnp.where(odd, cosine, sine)
    cos_value = jnp.where(((turn + 1) & 2) == 2, -cos_base, cos_base)
    sin_value = jnp.where((turn & 2) == 2, -sin_base, sin_base)
    return (cos_value, sin_value)


def phase_tile(places, vectors):
    angles = (
        places[0][:, None] * vectors[0][None, :]
        + places[1][:, None] * vectors[1][None, :]
        + places[2][:, None] * vectors[2][None, :]
    )
    cos_value, sin_value = sine_cosine(angles)
    return (cos_value.astype(jnp.bfloat16), sin_value.astype(jnp.bfloat16))


def field_terms(coef_block, cos_tile, sin_tile):
    order_count = coef_block.shape[0] // 2
    real_rows = coef_block[:order_count]
    imag_rows = coef_block[order_count:]
    top_rows = jnp.concatenate([real_rows, imag_rows], axis=1)
    low_rows = jnp.concatenate([imag_rows, -real_rows], axis=1)
    left_side = jnp.concatenate([top_rows, low_rows], axis=0)
    right_side = jnp.concatenate([cos_tile, sin_tile], axis=0)
    return jnp.dot(left_side, right_side, preferred_element_type=jnp.float32)


def adjoint_terms(stacked, cos_tile, sin_tile):
    order_count = stacked.shape[0] // 2
    real_rows = stacked[:order_count]
    imag_rows = stacked[order_count:]
    top_rows = jnp.concatenate([real_rows, imag_rows], axis=1)
    low_rows = jnp.concatenate([imag_rows, -real_rows], axis=1)
    left_side = jnp.concatenate([top_rows, low_rows], axis=0)
    right_side = jnp.concatenate([cos_tile, sin_tile], axis=1)
    return lax.dot_general(
        left_side, right_side, (((1,), (1,)), ((), ())), preferred_element_type=jnp.float32
    )


def amplitude_parts(fields, farmap):
    order_count = fields.shape[0] // 2
    field_real = fields[:order_count][None]
    field_imag = fields[order_count:][None]
    map_real = farmap[:, 0]
    map_imag = farmap[:, 1]
    amp_real = jnp.sum(map_real * field_real - map_imag * field_imag, axis=1)
    amp_imag = jnp.sum(map_real * field_imag + map_imag * field_real, axis=1)
    return (amp_real, amp_imag)


def cotangent_from(amp_real, amp_imag, farmap, weights):
    map_real = farmap[:, 0]
    map_imag = farmap[:, 1]
    cot_real = weights * jnp.sum(
        amp_real[:, None] * map_real + amp_imag[:, None] * map_imag, axis=0
    )
    cot_imag = weights * jnp.sum(
        amp_real[:, None] * map_imag - amp_imag[:, None] * map_real, axis=0
    )
    return jnp.concatenate([cot_real, cot_imag], axis=0).astype(jnp.bfloat16)


def cotangent_rows(fields, farmap, weights):
    amp_real, amp_imag = amplitude_parts(fields, farmap)
    return cotangent_from(amp_real, amp_imag, farmap, weights)


def stacked_rows(adjoint, vectors):
    order_count = adjoint.shape[0] // 2
    widened = adjoint.astype(jnp.float32)
    scaled = [(vectors[axis_id][None, :] * widened).astype(jnp.bfloat16) for axis_id in range(3)]
    real_parts = [adjoint[:order_count]] + [item[:order_count] for item in scaled]
    imag_parts = [adjoint[order_count:]] + [item[order_count:] for item in scaled]
    return jnp.concatenate(real_parts + imag_parts, axis=0)


def gradients(output, coef_block):
    order_count = coef_block.shape[0] // 2
    real_out = output[: 4 * order_count]
    imag_out = output[4 * order_count :]
    coef_term = jnp.concatenate(
        [2.0 * real_out[:order_count], -2.0 * imag_out[:order_count]], axis=0
    )
    coef_real = coef_block[:order_count].astype(jnp.float32)
    coef_imag = coef_block[order_count:].astype(jnp.float32)
    place_terms = []
    for axis_id in range(3):
        lower_row = (axis_id + 1) * order_count
        upper_row = (axis_id + 2) * order_count
        place_terms.append(
            2.0
            * jnp.sum(
                coef_real * imag_out[lower_row:upper_row]
                + coef_imag * real_out[lower_row:upper_row],
                axis=0,
            )
        )
    return (coef_term, jnp.stack(place_terms))


DOM_AXES = ("y", "z_lo", "core")
DIR_AXES = ("x", "z_hi")


def gather_blocks(block, axis_name, size):
    spread = jnp.broadcast_to(block[None], (size,) + block.shape)
    return lax.all_to_all(spread, axis_name, 0, 0, tiled=True)


def scatter_sum(part, axis_name, size, sum_type=None):
    rows, width = part.shape
    split = part.reshape(rows, size, width // size)
    received = lax.all_to_all(split, axis_name, 1, 1, tiled=True)
    return jnp.sum(received.astype(sum_type or received.dtype), axis=1)


def scatter_dir(part, sizes):
    rows, width = part.shape
    size = sizes[0] * sizes[1]
    split = part.reshape(rows, size, width // size)
    received = lax.all_to_all(narrow_rows(split), DIR_AXES, 1, 1, tiled=True)
    return jnp.sum(widen_rows(received), axis=1)


def narrow_rows(part):
    coef_rows = part[: 2 * C].astype(jnp.bfloat16)
    place_high = part[2 * C :].astype(jnp.bfloat16)
    place_low = (part[2 * C :] - place_high.astype(jnp.float32)).astype(jnp.bfloat16)
    return jnp.concatenate([coef_rows, place_high, place_low], axis=0)


def widen_rows(packed):
    wide = packed.astype(jnp.float32)
    place_count = (packed.shape[0] - 2 * C) // 2
    place_rows = wide[2 * C : 2 * C + place_count] + wide[2 * C + place_count :]
    return jnp.concatenate([wide[: 2 * C], place_rows], axis=0)


def body(coefficients, positions, polar, azimuth, weights, farmap, dir_sizes, dom_size):
    own_count = coefficients.shape[2]
    dir_size = dir_sizes[0] * dir_sizes[1]
    own_rows = coefficients.reshape(2 * C, own_count)
    place_high = positions.astype(jnp.bfloat16)
    place_rest = positions - place_high.astype(jnp.float32)
    place_mid = place_rest.astype(jnp.bfloat16)
    place_low = (place_rest - place_mid.astype(jnp.float32)).astype(jnp.bfloat16)
    packed = jnp.concatenate([own_rows, place_high, place_mid, place_low], axis=0)
    inner_blocks = gather_blocks(packed, DIR_AXES[1], dir_sizes[1])
    packed_blocks = gather_blocks(inner_blocks, DIR_AXES[0], dir_sizes[0]).reshape(
        (dir_size,) + packed.shape
    )
    domain_packed = jnp.moveaxis(packed_blocks, 0, 1).reshape(
        packed.shape[0], dir_size * own_count
    )
    domain_rows = domain_packed[: 2 * C]
    pieces = domain_packed[2 * C :].astype(jnp.float32)
    domain_places = pieces[0:3] + pieces[3:6] + pieces[6:9]
    vectors = unit_vectors(polar, azimuth)
    cos_tile, sin_tile = phase_tile(domain_places, vectors)
    partial_fields = field_terms(domain_rows, cos_tile, sin_tile)
    amp_real, amp_imag = amplitude_parts(partial_fields, farmap)
    amp_parts = gather_blocks(jnp.stack([amp_real, amp_imag]), DOM_AXES, dom_size)
    amp_total = jnp.sum(amp_parts, axis=0)
    adjoint = cotangent_from(amp_total[0], amp_total[1], farmap, weights)
    stacked = stacked_rows(adjoint, vectors)
    coef_part, place_part = gradients(adjoint_terms(stacked, cos_tile, sin_tile), domain_rows)
    part = jnp.concatenate([coef_part, place_part], axis=0)
    reduced = scatter_dir(part, dir_sizes)
    return (reduced[: 2 * C].reshape(2, C, own_count), reduced[2 * C :])


def solution(mesh):
    dom_size = mesh.shape["dom"]
    dir_size = mesh.shape["dir"]
    chips_z = 2 if dom_size % 4 == 0 else 1
    dom_sizes = (dom_size // (2 * chips_z), chips_z, 2)
    x_size = 4 if dir_size % 4 == 0 else dir_size
    dir_sizes = (x_size, dir_size // x_size)
    fine = jax.sharding.Mesh(
        mesh.devices.reshape(dom_sizes + dir_sizes), DOM_AXES + DIR_AXES
    )
    every = DOM_AXES + DIR_AXES
    placed = (
        P(None, None, every),
        P(None, every),
        P(DIR_AXES),
        P(DIR_AXES),
        P(DIR_AXES),
        P(None, None, None, DIR_AXES),
    )
    return jax.shard_map(
        functools.partial(body, dir_sizes=dir_sizes, dom_size=dom_size),
        mesh=fine,
        in_specs=placed,
        out_specs=(P(None, None, every), P(None, every)),
        check_vma=False,
    )
```
